32 devices in a mesh: expert: 8 (over z, x), shard: 4 (over y, core).
Axes of the slice: x: 2, y: 2, z: 4, core: 2. Of those that a mesh axis runs over, the one named last changes fastest.
Arguments:
- tokens: bfloat16 [2, 3072, 2048], P(None, ('expert', 'shard')), may hold values from -6 to 6
- cotangent: bfloat16 [2, 3072, 2048], P(None, ('expert', 'shard')), may hold values from -6 to 6
- block_ids: int32 [2, 8, 384], P(None, 'expert'), may hold values from 0 to 2, never falling along the last dimension, each value on 1 to 256 neighbouring positions
- routes: int32 [2, 3072, 8], P(None, ('expert', 'shard')), may hold values from 0 to 15, all different within a row; in each aligned block of 96 rows (0 to 95, 96 to 191, ..., all dimensions but the last counted through in order) at most 54 rows name the same one
- w_query: bfloat16 [2048, 2048], P(('expert', 'shard')), may hold values from -0.125 to 0.125
- w_key: bfloat16 [2048, 2048], P(('expert', 'shard')), may hold values from -0.125 to 0.125
- w_value: bfloat16 [2048, 2048], P(('expert', 'shard')), may hold values from -0.125 to 0.125
- w_out: bfloat16 [2048, 2048], P(('expert', 'shard')), may hold values from -1.5 to 1.5
- router: bfloat16 [2048, 16], P(('expert', 'shard')), may hold values from -0.0625 to 0.0625
- attention_gain: bfloat16 [2048], P(('expert', 'shard')), may hold values from 0.099609375 to 1.8984375
- query_gain: bfloat16 [2048], P(('expert', 'shard')), may hold values from 0.099609375 to 1.8984375
- key_gain: bfloat16 [2048], P(('expert', 'shard')), may hold values from 0.099609375 to 1.8984375
- mixture_gain: bfloat16 [2048], P(('expert', 'shard')), may hold values from 0.099609375 to 1.8984375
- w_gate: bfloat16 [16, 2048, 1024], P('expert', 'shard'), may hold values from -0.125 to 0.125
- w_up: bfloat16 [16, 2048, 1024], P('expert', 'shard'), may hold values from -0.125 to 0.125
- w_down: bfloat16 [16, 1024, 2048], P('expert', 'shard'), may hold values from -6 to 6
Outputs:
- output: bfloat16 [2, 3072, 2048], P(None, ('expert', 'shard'))
- input_grad: bfloat16 [2, 3072, 2048], P(None, ('expert', 'shard'))
- w_query_grad: float32 [2048, 2048], P(('expert', 'shard'))
- w_key_grad: float32 [2048, 2048], P(('expert', 'shard'))
- w_value_grad: float32 [2048, 2048], P(('expert', 'shard'))
- w_out_grad: float32 [2048, 2048], P(('expert', 'shard'))
- router_grad: float32 [2048, 16], P(('expert', 'shard'))
- attention_gain_grad: float32 [2048], P(('expert', 'shard'))
- query_gain_grad: float32 [2048], P(('expert', 'shard'))
- key_gain_grad: float32 [2048], P(('expert', 'shard'))
- mixture_gain_grad: float32 [2048], P(('expert', 'shard'))
- w_gate_grad: float32 [16, 2048, 1024], P('expert', 'shard')
- w_up_grad: float32 [16, 2048, 1024], P('expert', 'shard')
- w_down_grad: float32 [16, 1024, 2048], P('expert', 'shard')
The draws below stay inside these ranges and needn't reach their ends.
Inputs may be any that keep to these rules, and one draw needn't show every extreme that they name: `routes`: each token names 8 different experts. In the rows of one device in one micro-batch (aligned blocks of 96 rows) no expert is named more than 54 times, and in some such block one expert exactly 54 times. `block_ids`: along each sequence the block numbers never fall; each block holds 1 to 256 positions, one block exactly 256.
All inputs are finite; a program needn't handle non-finite values.
Results may differ from the reference program's by a relative error of at most 0.022.
Values may be sent and summed in bfloat16 or wider, within the bound.
No kernel may reach another device: no remote copies, remote signals or barrier semaphores. Data moves between devices by JAX's collectives and lax.ppermute only.
A program may use at most 384 MiB of HBM per device.

```python
import math
import jax
import jax.numpy as jnp
import numpy as np
from jax import lax

D = 2048
HEADS = 16
HEAD_DIM = 128
FF = 1024
TOPK = 8
MICRO = 2
BLOCK = 256
TOK_MB = 96
EXPERTS = 16
CAP = 54
LEN = 384
NBLK = 3
SEQS = 8
TOKENS_MB = 3072
DEVICES = 32


def shard_levels(rng, shape, cuts, least, top_value):
    factor_of, own = 1.0, jax.random.fold_in(rng, 6)
    for axis_at, shards_of in cuts:
        steps = jnp.exp(jax.random.uniform(jax.random.fold_in(own, axis_at), (shards_of,), jnp.float32, least / len(cuts), top_value / len(cuts)))
        factor_of = factor_of * jnp.repeat(steps, shape[axis_at] // shards_of).reshape([-1 if axis == axis_at else 1 for axis in range(len(shape))])
    return factor_of


def split_up(count, total, most, slope):
    portions = [(1 << 20) // math.isqrt(grade ** slope) + 1 for grade in range(2, count + 1)]
    surplus, given = total - most - (count - 1), [1] * (count - 1)
    while surplus > 0:
        movable = [i for i in range(count - 1) if given[i] < most]
        pool, remaining = sum([portions[i] for i in movable]), surplus
        for i in movable:
            more = min(most - given[i], max(1, remaining * portions[i] // pool), surplus)
            given[i] = given[i] + more
            surplus = surplus - more
    return np.array([most] + given)


def uneven(stream_key, count, total, limit, skew):
    if count == 2:
        one = jax.random.randint(stream_key, (), max(1, total - limit), min(limit, total - 1) + 1)
        return jnp.stack([one, total - one])
    sizes = jnp.asarray(split_up(count, total, limit, skew), jnp.int32)
    pairs = (count - 1) // 2
    donor, sink = sizes[1:1 + 2 * pairs:2], sizes[2:2 + 2 * pairs:2]
    slack = jnp.minimum(donor - 1, limit - sink)
    moved = jax.random.randint(jax.random.fold_in(stream_key, 1), (pairs,), 0, 1 << 20) % (slack + 1)
    sizes = sizes.at[1:1 + 2 * pairs:2].set(donor - moved).at[2:2 + 2 * pairs:2].set(sink + moved)
    return sizes[jax.random.permutation(jax.random.fold_in(stream_key, 2), count)]


def routed_block(own_key, own, number, rows, amount, top, reach, slope):
    sequence = jax.random.permutation(own_key, amount)
    crowded, ordinary = portions_of(amount, rows * top, reach, slope, True), portions_of(amount, rows * top, reach, slope, False)
    places = jnp.arange(amount)

    def named(lengths, turn):
        used = int((lengths > 0).sum())
        fixed = max(1, used // 4)
        shifted = fixed + (places - fixed + turn * (used - fixed)) % max(1, amount - fixed)
        return jnp.zeros((amount,), jnp.int32).at[sequence[jnp.where(places < fixed, places, shifted)]].set(jnp.asarray(lengths, jnp.int32))

    lengths = jnp.where(number % 4 == 0, named(crowded, number // 4), named(ordinary, number - number // 4 - 1))
    mixed = jax.random.permutation(jax.random.fold_in(own, 3), amount)
    giver, receiver = mixed[0:amount // 2 * 2:2], mixed[1:amount // 2 * 2:2]
    slack = jnp.minimum(lengths[giver] - 1, reach - lengths[receiver]) // 2
    slack = jnp.where((giver == sequence[0]) | (receiver == sequence[0]) | (lengths[receiver] == 0), 0, jnp.maximum(slack, 0))
    shifted = jax.random.randint(jax.random.fold_in(own, 4), (amount // 2,), 0, 1 << 20) % (slack + 1)
    lengths = lengths.at[giver].add(-shifted).at[receiver].add(shifted)
    labels = jnp.searchsorted(jnp.cumsum(lengths), jnp.arange(rows * top), side="right").astype(jnp.int32)
    grid = labels.reshape(top, rows).T
    grid = grid[jax.random.permutation(jax.random.fold_in(own, 1), rows)]
    turn = jax.random.randint(jax.random.fold_in(own, 2), (rows, 1), 0, top)
    return jnp.take_along_axis(grid, (jnp.arange(top)[None, :] + turn) % top, axis=1)


def portions_of(count, total, most, skew, full):
    portions = [(1 << 20) // math.isqrt(standing ** skew) + 1 for standing in range(1, count + 1)]
    largest = most if full else min(most, max(-(-total // count), total * portions[0] // sum(portions)))
    least = 1 if total - largest >= count - 1 else 0
    given, spare = [largest] + [least] * (count - 1), total - largest - least * (count - 1)
    while spare > 0:
        candidates = [i for i in range(1, count) if given[i] < largest] or [i for i in range(1, count) if given[i] < most]
        whole, left = sum([portions[i] for i in candidates]), spare
        for i in candidates:
            more = min(most - given[i], max(1, left * portions[i] // whole), spare)
            given[i] = given[i] + more
            spare = spare - more
    return np.array(given)


def normal_values(stream_key, shape, width, reach, split=(), kind=jnp.bfloat16):
    values = width * jax.random.normal(stream_key, shape, jnp.float32)
    if split:
        values = values * shard_levels(stream_key, shape, split, -0.22, 0.18)
    return jnp.clip(values, -reach, reach).astype(kind)


def setup_inputs(seed: int = 0) -> dict:
    key_list = jax.random.split(jax.random.key(seed), 17)
    tokens = normal_values(key_list[0], (MICRO, TOKENS_MB, D), 1.0, 6.0, ((1, 32),))
    cotangent = normal_values(key_list[1], (MICRO, TOKENS_MB, D), 1.0, 6.0, ((1, 32),))
    block_ids = jax.vmap(lambda own: jnp.searchsorted(jnp.cumsum(uneven(own, NBLK, LEN, BLOCK, 1)), jnp.arange(LEN), side="right"))(jax.random.split(key_list[2], MICRO * SEQS)).reshape((MICRO, SEQS, LEN)).astype(jnp.int32)
    routes_keys = jax.random.split(jax.random.fold_in(key_list[3], 1), MICRO * TOKENS_MB // TOK_MB)
    routes_turns = jax.random.permutation(jax.random.fold_in(key_list[3], 3), MICRO * TOKENS_MB // TOK_MB)
    routes = jax.vmap(lambda own, number: routed_block(jax.random.fold_in(key_list[3], 2), own, number, TOK_MB, EXPERTS, TOPK, CAP, 2))(routes_keys, routes_turns).reshape((MICRO, TOKENS_MB, TOPK))
    w_query = normal_values(key_list[4], (D, D), D ** -0.5, 0.125, ((0, 32),))
    w_key = normal_values(key_list[5], (D, D), D ** -0.5, 0.125, ((0, 32),))
    w_value = normal_values(key_list[6], (D, D), D ** -0.5, 0.125, ((0, 32),))
    w_out = normal_values(key_list[7], (D, D), (D // 128) ** -0.5, 1.5, ((0, 32),))
    router = normal_values(key_list[8], (D, EXPERTS), (4 * D) ** -0.5, 0.0625, ((0, 32),))
    attention_gain = jnp.clip(1.0 + 0.18 * jax.random.normal(key_list[9], (D,), jnp.float32), 0.099609375, 1.8984375).astype(jnp.bfloat16)
    query_gain = jnp.clip(1.0 + 0.18 * jax.random.normal(key_list[10], (D,), jnp.float32), 0.099609375, 1.8984375).astype(jnp.bfloat16)
    key_gain = jnp.clip(1.0 + 0.18 * jax.random.normal(key_list[11], (D,), jnp.float32), 0.099609375, 1.8984375).astype(jnp.bfloat16)
    mixture_gain = jnp.clip(1.0 + 0.18 * jax.random.normal(key_list[12], (D,), jnp.float32), 0.099609375, 1.8984375).astype(jnp.bfloat16)
    w_gate = normal_values(key_list[13], (EXPERTS, D, FF), D ** -0.5, 0.125, ((0, 8), (1, 4)))
    w_up = normal_values(key_list[14], (EXPERTS, D, FF), D ** -0.5, 0.125, ((0, 8), (1, 4)))
    w_down = normal_values(key_list[15], (EXPERTS, FF, D), (max(1, FF // 1024)) ** -0.5, 6.0, ((0, 8), (1, 4)))
    return {"tokens": tokens, "cotangent": cotangent, "block_ids": block_ids, "routes": routes, "w_query": w_query, "w_key": w_key, "w_value": w_value, "w_out": w_out, "router": router, "attention_gain": attention_gain, "query_gain": query_gain, "key_gain": key_gain, "mixture_gain": mixture_gain, "w_gate": w_gate, "w_up": w_up, "w_down": w_down}


epsilon = 1e-05
rope_base = 10000.0
masked_value = -1e+30

@jax.custom_vjp
def low(v):
    return lax.optimization_barrier(v.astype(jnp.bfloat16)).astype(jnp.float32)

@jax.custom_vjp
def low_back(v):
    return v

def low_keep(v):
    return (low(v), None)

def low_pass(kept, grad):
    return (grad,)

def back_keep(v):
    return (v, None)

def back_low(kept, grad):
    return (low(grad),)
low.defvjp(low_keep, low_pass)
low_back.defvjp(back_keep, back_low)

def matmul_high(left, right):
    return jnp.dot(left, right, precision=lax.Precision.HIGHEST, preferred_element_type=jnp.float32)

def rms_scale(values, gain_row):
    return values * lax.rsqrt(lax.optimization_barrier(jnp.mean(values * values, axis=-1, keepdims=True)) + epsilon) * gain_row

def rotate(values, positions):
    half_dim = values.shape[-1] // 2
    inverse_rate = rope_base ** (-2.0 * jnp.arange(half_dim, dtype=jnp.float32) / values.shape[-1])
    angles = positions.astype(jnp.float32)[:, None] * inverse_rate[None, :]
    cosine = jnp.cos(angles)[:, None, :]
    sine_part = jnp.sin(angles)[:, None, :]
    first_half = values[..., :half_dim]
    second_half = values[..., half_dim:]
    return jnp.concatenate([first_half * cosine - second_half * sine_part, second_half * cosine + first_half * sine_part], axis=-1)

def attend(normed, blocks, w_query, w_key, w_value, query_gain, key_gain):
    length = normed.shape[0]
    positions = jnp.arange(length, dtype=jnp.int32)
    query_linear = low_back(matmul_high(normed, w_query))
    key_linear = low_back(matmul_high(normed, w_key))
    value_linear = low_back(matmul_high(normed, w_value))
    query_turned = low(rotate(rms_scale(query_linear, query_gain).reshape(length, HEADS, HEAD_DIM), positions))
    key_turned = low(rotate(rms_scale(key_linear, key_gain).reshape(length, HEADS, HEAD_DIM), positions))
    value_rows = low(value_linear).reshape(length, HEADS, HEAD_DIM)
    scores = low_back(jnp.einsum('qhd,khd->hqk', query_turned, key_turned, precision=lax.Precision.HIGHEST) * HEAD_DIM ** (-0.5))
    visible = blocks[None, :] <= blocks[:, None]
    scores = jnp.where(visible[None, :, :], scores, masked_value)
    softmax_rows = jax.nn.softmax(scores, axis=-1)
    attended = jnp.einsum('hqk,khd->qhd', low(softmax_rows), value_rows, precision=lax.Precision.HIGHEST)
    return low(low_back(attended.reshape(length, HEADS * HEAD_DIM)))

def slot_table_of(route_now):
    pair_expert = route_now.reshape(-1).astype(jnp.int32)
    pair_count = pair_expert.shape[0]
    member = (pair_expert[:, None] == jnp.arange(EXPERTS, dtype=jnp.int32)[None, :]).astype(jnp.int32)
    rank_before = jnp.cumsum(member, axis=0).astype(jnp.int32) - member
    slot_index = lax.optimization_barrier(jnp.sum(rank_before * member, axis=1)).astype(jnp.int32)
    flat_table = jnp.full((EXPERTS * DEVICES * CAP,), pair_count, jnp.int32)
    flat_table = flat_table.at[pair_expert * (DEVICES * CAP) + slot_index].set(jnp.arange(pair_count, dtype=jnp.int32))
    return flat_table.reshape(EXPERTS, DEVICES * CAP)

def layer(inputs, w_query, w_key, w_value, w_out, router, attention_gain, query_gain, key_gain, mixture_gain, w_gate, w_up, w_down, blocks, route_now, slot_table):
    rows_all = inputs.shape[0]
    attention_in = low(rms_scale(inputs, attention_gain))

    def one_sequence(element):
        return attend(element[0], element[1], w_query, w_key, w_value, query_gain, key_gain)
    attended = lax.map(jax.checkpoint(one_sequence), (attention_in.reshape(SEQS, LEN, D), blocks))
    branch = low_back(matmul_high(attended.reshape(rows_all, D), w_out))
    hidden_state = inputs + branch
    mixture_in = low(rms_scale(hidden_state, mixture_gain))
    logits = low_back(matmul_high(mixture_in, router))
    gate_values = jnp.take_along_axis(jax.nn.softmax(logits, axis=-1), route_now, axis=1)
    pair_count = rows_all * TOPK
    token_table = jnp.where(slot_table < pair_count, slot_table // TOPK, rows_all).astype(jnp.int32)
    padded_in = jnp.concatenate([mixture_in, jnp.zeros((1, D), jnp.float32)], axis=0)
    padded_gate = jnp.concatenate([gate_values.reshape(-1), jnp.zeros((1,), jnp.float32)], axis=0)

    def one_expert(element):
        token_index, gate_weight, up_weight, down_weight = element
        rows_in = low_back(padded_in[token_index])
        gate_linear = low_back(matmul_high(rows_in, gate_weight))
        up_linear = low_back(matmul_high(rows_in, up_weight))
        inner_values = low(jax.nn.silu(gate_linear) * up_linear)
        return low(low_back(matmul_high(inner_values, down_weight)))
    expert_rows = lax.map(jax.checkpoint(one_expert), (token_table, w_gate, w_up, w_down))
    scaled = padded_gate[slot_table][..., None] * expert_rows
    combined = jnp.zeros((rows_all + 1, D), jnp.float32).at[token_table.reshape(-1)].add(scaled.reshape(-1, D))
    return hidden_state + combined[:rows_all]

def reference(tokens, cotangent, block_ids, routes, w_query, w_key, w_value, w_out, router, attention_gain, query_gain, key_gain, mixture_gain, w_gate, w_up, w_down):
    weights = tuple((element.astype(jnp.float32) for element in (w_query, w_key, w_value, w_out, router, attention_gain, query_gain, key_gain, mixture_gain, w_gate, w_up, w_down)))
    totals = tuple((jnp.zeros(element.shape, jnp.float32) for element in weights))
    outputs = []
    input_grads = []
    for micro_index in range(MICRO):
        route_now = routes[micro_index]
        slot_table = slot_table_of(route_now)
        blocks = block_ids[micro_index]

        def forward(inputs, *params):
            return layer(inputs, *params, blocks, route_now, slot_table)
        result, pullback = jax.vjp(forward, tokens[micro_index].astype(jnp.float32), *weights)
        gradients = pullback(cotangent[micro_index].astype(jnp.float32))
        outputs.append(result.astype(jnp.bfloat16))
        input_grads.append(gradients[0].astype(jnp.bfloat16))
        totals = tuple((total_now + grad_now for total_now, grad_now in zip(totals, gradients[1:])))
    return (jnp.stack(outputs), jnp.stack(input_grads), totals[0], totals[1], totals[2], totals[3], totals[4], totals[5], totals[6], totals[7], totals[8], totals[9], totals[10], totals[11])
```

```python
import jax
import jax.numpy as jnp
from jax import lax
from jax.experimental import pallas as pl
from jax.experimental.pallas import tpu as pltpu
from jax.sharding import PartitionSpec as P

HEADS = 16
HEAD_DIM = 128
EPSILON = 1e-05
ROPE_BASE = 10000.0
MASKED = -1e30
BOTH = ("expert", "shard")

f32 = jnp.float32
bf16 = jnp.bfloat16


def dot(left, right, dims):
    return lax.dot_general(left, right, (dims, ((), ())), preferred_element_type=f32)


def nn(left, right):
    return dot(left, right, ((1,), (0,)))


def nt(left, right):
    return dot(left, right, ((1,), (1,)))


def tn(left, right):
    return dot(left, right, ((0,), (0,)))


def swap_core(values):
    return lax.ppermute(values, "shard", [(s, s ^ 1) for s in range(4)])


def swap_side(values):
    return lax.ppermute(values, "shard", [(s, s ^ 2) for s in range(4)])


def gather_shard(values):
    near = swap_core(values)
    far = swap_side(values)
    return [values, near, far, swap_core(far)]


def scatter_shard(parts):
    near = swap_core(jnp.stack([parts[1], parts[3]]).astype(bf16)).astype(f32)
    far = swap_side((parts[2] + near[1]).astype(bf16)).astype(f32)
    return parts[0] + near[0] + far


def tie(*values):
    return lax.optimization_barrier(values)


def sum_rows(values, core, side, tok):
    def reorder(v):
        v = v.reshape(2, -1, 2, 2, tok)
        v = jnp.where(core == 1, jnp.concatenate([v[:, :, :, 1:], v[:, :, :, :1]], axis=3), v)
        v = jnp.where(side == 1, jnp.concatenate([v[:, :, 1:], v[:, :, :1]], axis=2), v)
        return v.reshape(values.shape)

    return reorder(jnp.sum(lax.all_gather(reorder(values), "shard", axis=0), axis=0))


def inverse_rms(values):
    return lax.rsqrt(jnp.mean(values * values, axis=-1, keepdims=True) + EPSILON)


def attend_body(q_ref, k_ref, v_ref, qi_ref, ki_ref, gq_ref, gk_ref, cos_ref, sin_ref, idq_ref, idk_ref,
                qr_ref, kr_ref, vr_ref, o_ref, lse_ref):
    cos = cos_ref[...]
    sin = sin_ref[...]
    half = HEAD_DIM // 2

    def rope(values):
        return (values * cos + pltpu.roll(values, half, 1) * sin).astype(bf16)

    q_r = rope(q_ref[...] * qi_ref[...] * gq_ref[...])
    k_r = rope(k_ref[...] * ki_ref[...] * gk_ref[...])
    v_r = v_ref[...].astype(bf16)
    qr_ref[...] = q_r
    kr_ref[...] = k_r
    vr_ref[...] = v_r
    scores = jnp.where(idk_ref[0] <= idq_ref[...], nt(q_r, k_r) * HEAD_DIM ** (-0.5), MASKED)
    peak = jnp.max(scores, axis=-1, keepdims=True)
    weight = jnp.exp(scores - peak)
    total = jnp.sum(weight, axis=-1, keepdims=True)
    o_ref[...] = nn((weight / total).astype(bf16), v_r).astype(bf16)
    lse_ref[0] = peak + jnp.log(total)


def attend(linear, q_inv, k_inv, gain_q, gain_k, cos, sin, ids, heads):
    micro, length = ids.shape
    cols = heads * HEAD_DIM
    total = micro * length
    head = lambda base: pl.BlockSpec((length, HEAD_DIM), lambda m, h: (m, base + h))
    column = pl.BlockSpec((length, 1), lambda m, h: (m, 0))
    gain = pl.BlockSpec((1, HEAD_DIM), lambda m, h: (0, h))
    angle = pl.BlockSpec((length, HEAD_DIM), lambda m, h: (0, 0))
    keys = pl.BlockSpec((1, 1, length), lambda m, h: (m, 0, 0))
    low = jax.ShapeDtypeStruct((total, cols), bf16)
    return pl.pallas_call(
        attend_body,
        grid=(micro, heads),
        in_specs=[head(0), head(heads), head(2 * heads), column, column, gain, gain, angle, angle, column, keys],
        out_specs=[head(0)] * 4 + [pl.BlockSpec((1, length, 1), lambda m, h: (m * heads + h, 0, 0))],
        out_shape=[low] * 4 + [jax.ShapeDtypeStruct((micro * heads, length, 1), f32)],
    )(linear, linear, linear, q_inv, k_inv, gain_q, gain_k, cos, sin, ids.reshape(total, 1), ids[:, None, :])


def attend_back_body(dh_ref, wo_ref, q_ref, k_ref, qr_ref, kr_ref, vr_ref, lse_ref, qi_ref, ki_ref, gq_ref, gk_ref,
                     cos_ref, sin_ref, idq_ref, idk_ref, wq_ref, wk_ref, dv_ref, pq_ref, pk_ref, sum_ref):
    cos = cos_ref[...]
    sin = sin_ref[...]
    half = HEAD_DIM // 2
    scale = HEAD_DIM ** (-0.5)
    q_r = qr_ref[...]
    k_r = kr_ref[...]
    d_o = nt(dh_ref[...], wo_ref[...]).astype(bf16)
    scores = jnp.where(idk_ref[0] <= idq_ref[...], nt(q_r, k_r) * scale, MASKED)
    prob = jnp.exp(scores - lse_ref[0])
    d_prob = nt(d_o, vr_ref[...])
    delta = jnp.sum(prob * d_prob, axis=-1, keepdims=True)
    d_s = (prob * (d_prob - delta)).astype(bf16)
    dv_ref[...] = tn(prob.astype(bf16), d_o).astype(bf16)
    ones = jnp.ones((8, HEAD_DIM), f32)

    def finish(grad, linear, inverse, gain, out_ref, part_ref, at):
        grad = grad * scale
        grad = grad * cos - pltpu.roll(grad, half, 1) * sin
        normed = linear * inverse
        part_ref[...] = jnp.sum(grad * normed, axis=0, keepdims=True)
        grad = grad * gain
        out_ref[...] = grad
        rows = lax.dot_general(
            ones, grad * normed, (((1,), (1,)), ((), ())), precision=lax.Precision.HIGHEST, preferred_element_type=f32
        )

        @pl.when(pl.program_id(0) == 0)
        def _():
            sum_ref[at] = rows

        @pl.when(pl.program_id(0) > 0)
        def _():
            sum_ref[at] = sum_ref[at] + rows

    finish(nn(d_s, k_r), q_ref[...], qi_ref[...], gq_ref[...], wq_ref, pq_ref, 0)
    finish(tn(d_s, q_r), k_ref[...], ki_ref[...], gk_ref[...], wk_ref, pk_ref, 1)


def attend_back(m, dh, w_o, linear, q_r, k_r, v_r, lse, q_inv, k_inv, gain_q, gain_k, cos, sin, ids, heads):
    micro, length = ids.shape
    cols = heads * HEAD_DIM
    width = dh.shape[1]
    head = lambda base: pl.BlockSpec((length, HEAD_DIM), lambda h: (m, base + h))
    column = pl.BlockSpec((length, 1), lambda h: (m, 0))
    gain = pl.BlockSpec((1, HEAD_DIM), lambda h: (0, h))
    angle = pl.BlockSpec((length, HEAD_DIM), lambda h: (0, 0))
    keys = pl.BlockSpec((1, 1, length), lambda h: (m, 0, 0))
    out = pl.BlockSpec((length, HEAD_DIM), lambda h: (0, h))
    return pl.pallas_call(
        attend_back_body,
        grid=(heads,),
        in_specs=[
            pl.BlockSpec((length, width), lambda h: (0, 0)),
            pl.BlockSpec((HEAD_DIM, width), lambda h: (h, 0)),
            head(0), head(heads), head(0), head(0), head(0),
            pl.BlockSpec((1, length, 1), lambda h: (m * heads + h, 0, 0)),
            column, column, gain, gain, angle, angle, column, keys,
        ],
        out_specs=[out, out, out, gain, gain, pl.BlockSpec((2, 8, length), lambda h: (0, 0, 0))],
        out_shape=[
            jax.ShapeDtypeStruct((length, cols), f32),
            jax.ShapeDtypeStruct((length, cols), f32),
            jax.ShapeDtypeStruct((length, cols), bf16),
            jax.ShapeDtypeStruct((1, cols), f32),
            jax.ShapeDtypeStruct((1, cols), f32),
            jax.ShapeDtypeStruct((2, 8, length), f32),
        ],
    )(dh, w_o, linear, linear, q_r, k_r, v_r, lse, q_inv, k_inv, gain_q, gain_k, cos, sin,
      ids.reshape(micro * length, 1), ids[:, None, :])


def project_back_body(wq_ref, wk_ref, dv_ref, q_ref, k_ref, qi_ref, ki_ref, sq_ref, sk_ref, out_ref):
    cols = wq_ref.shape[1]
    q_inv = qi_ref[...]
    k_inv = ki_ref[...]
    out_ref[:, :cols] = (q_inv * (wq_ref[...] - q_ref[...] * (q_inv * sq_ref[...]))).astype(bf16)
    out_ref[:, cols : 2 * cols] = (k_inv * (wk_ref[...] - k_ref[...] * (k_inv * sk_ref[...]))).astype(bf16)
    out_ref[:, 2 * cols :] = dv_ref[...]


def project_back(m, w_q, w_k, d_v, linear, q_inv, k_inv, s_q, s_k):
    length, cols = w_q.shape
    rows = length // 2
    full = pl.BlockSpec((rows, cols), lambda i: (i, 0))
    column = pl.BlockSpec((rows, 1), lambda i: (2 * m + i, 0))
    own = pl.BlockSpec((rows, 1), lambda i: (i, 0))
    return pl.pallas_call(
        project_back_body,
        grid=(2,),
        in_specs=[full, full, full]
        + [pl.BlockSpec((rows, cols), lambda i, b=b: (2 * m + i, b)) for b in range(2)]
        + [column, column, own, own],
        out_specs=pl.BlockSpec((rows, 3 * cols), lambda i: (i, 0)),
        out_shape=jax.ShapeDtypeStruct((length, 3 * cols), bf16),
    )(w_q, w_k, d_v, linear, linear, q_inv, k_inv, s_q, s_k)


def half_expert(weight, core):
    other = lax.dynamic_index_in_dim(weight, 1 - core, 0, keepdims=True)
    return lax.dynamic_update_slice(weight, swap_core(other), (1 - core, 0, 0))


def whole_expert(half, side):
    far = swap_side(half)
    whole = jnp.concatenate([half, half], axis=0)
    whole = lax.dynamic_update_slice(whole, far, (2 * (1 - side), 0, 0))
    return whole.reshape(4 * half.shape[1], half.shape[2])


def send_side(grad, side):
    grad = grad.reshape(4, grad.shape[0] // 4, grad.shape[1])
    return swap_side(lax.dynamic_slice_in_dim(grad, 2 * (1 - side), 2, 0).astype(bf16))


def share_expert_grad(grad, far, core, side):
    grad = grad.reshape(4, grad.shape[0] // 4, grad.shape[1])
    mine = lax.dynamic_slice_in_dim(grad, 2 * side, 2, 0) + far.astype(f32)
    near = swap_core(lax.dynamic_index_in_dim(mine, 1 - core, 0, keepdims=True).astype(bf16))
    return lax.dynamic_update_slice(mine, near.astype(f32), (1 - core, 0, 0))


def local(
    tokens,
    cotangent,
    block_ids,
    routes,
    w_query,
    w_key,
    w_value,
    w_out,
    router,
    attention_gain,
    query_gain,
    key_gain,
    mixture_gain,
    w_gate,
    w_up,
    w_down,
):
    micro, tok, width = tokens.shape
    owners = lax.axis_size("expert")
    experts = router.shape[1]
    capacity = (tok * routes.shape[2] * 9 + 8 * experts - 1) // (8 * experts)
    pack = (2 * capacity + 15) // 16 * 16
    rows = w_query.shape[0]
    cols = width // 4
    heads = HEADS // 4
    length = 4 * tok
    s_index = lax.axis_index("shard")
    e_index = lax.axis_index("expert")
    core = s_index % 2
    side = s_index // 2
    my_expert = 2 * e_index + core

    top = routes.shape[2]
    route_cols = micro * tok * top // rows
    used = 4 + experts + route_cols
    aux_cols = (used + 127) // 128 * 128
    aux = jnp.concatenate(
        [
            jnp.stack([attention_gain, query_gain, key_gain, mixture_gain], axis=1),
            router,
            routes.astype(bf16).transpose(0, 2, 1).reshape(rows, route_cols),
            jnp.zeros((rows, aux_cols - used), bf16),
        ],
        axis=1,
    )
    blocks = [w.reshape(rows, 4, cols) for w in (w_query, w_key, w_value)]
    blocks.append(jnp.broadcast_to(aux[:, None, :], (rows, 4, aux_cols)))
    payload = jnp.concatenate(blocks, axis=2).transpose(1, 0, 2)
    half_gate = half_expert(w_gate, core)
    half_up = half_expert(w_up, core)
    payload, half_gate, half_up = tie(payload, half_gate, half_up)
    payload = lax.all_to_all(payload, "shard", split_axis=0, concat_axis=0, tiled=True)
    front = lax.all_gather(payload.reshape(4 * rows, 3 * cols + aux_cols), "expert", axis=0, tiled=True)
    devices = 4 * owners
    moves = [(b, (b % owners) * 4 + b // owners) for b in range(devices)]
    w_o = lax.all_gather(lax.ppermute(w_out, BOTH, moves), "expert", axis=0, tiled=True)

    gate_w = whole_expert(half_gate, side)
    up_w = whole_expert(half_up, side)
    down_w = whole_expert(half_expert(w_down, core), side)
    chunks = gather_shard(tokens)
    front, gate_w, up_w, *chunks = tie(front, gate_w, up_w, *chunks)
    w_qkv = front[:, : 3 * cols]
    aux_rows = front[:, 3 * cols :].T.astype(f32)
    gain_attention = aux_rows[0]
    gain_query = lax.dynamic_slice_in_dim(aux_rows[1], s_index * cols, cols)
    gain_key = lax.dynamic_slice_in_dim(aux_rows[2], s_index * cols, cols)
    gain_mixture = aux_rows[3]
    router_all = front[:, 3 * cols + 4 : 3 * cols + 4 + experts]


    all_routes = front[:, 3 * cols + 4 + experts : 3 * cols + used].astype(jnp.int32)
    all_routes = all_routes.reshape(owners, 4, micro, top, tok)
    mine = all_routes == my_expert
    mine = jnp.any(mine, axis=3)
    pair = [lax.dynamic_index_in_dim(mine, s_index ^ j, 1, keepdims=False) for j in range(2)]
    mask = jnp.concatenate(pair, axis=2).transpose(1, 0, 2)
    order = jnp.arange(2 * tok)
    earlier = (order[:, None] < order[None, :]).astype(bf16)
    slot = jnp.einsum("met,tu->meu", mask.astype(bf16), earlier, preferred_element_type=f32)
    slot = jnp.where(mask, slot.astype(jnp.int32), -1)
    chosen = (slot[:, :, None, :] == jnp.arange(pack)[None, None, :, None]).astype(bf16)

    x_all = jnp.concatenate(chunks, axis=1).reshape(micro * length, width).astype(f32)
    x_scale = inverse_rms(x_all)
    a_all = (x_all * x_scale * gain_attention).astype(bf16)
    linear = nn(a_all, w_qkv)
    q_lin = linear[:, :cols]
    k_lin = linear[:, cols : 2 * cols]
    sums = jnp.stack([jnp.sum(q_lin * q_lin, axis=1), jnp.sum(k_lin * k_lin, axis=1)])
    sums = sum_rows(sums, core, side, tok)
    inv = lax.rsqrt(sums / width + EPSILON)
    q_inv = inv[0][:, None]
    k_inv = inv[1][:, None]
    chunk_ids = [jnp.bitwise_xor(s_index, j) for j in range(4)]
    positions = jnp.concatenate([c * tok + jnp.arange(tok, dtype=jnp.int32) for c in chunk_ids])
    rate = ROPE_BASE ** (-2.0 * jnp.arange(HEAD_DIM // 2, dtype=f32) / HEAD_DIM)
    angles = positions.astype(f32)[:, None] * rate[None, :]
    cosine = jnp.cos(angles)
    sine = jnp.sin(angles)
    cosine = jnp.concatenate([cosine, cosine], axis=1)
    sine = jnp.concatenate([-sine, sine], axis=1)
    ids = block_ids[:, 0, :]
    ids = jnp.concatenate(
        [lax.dynamic_slice_in_dim(ids, c * tok, tok, axis=1) for c in chunk_ids], axis=1
    )
    gain_query = gain_query[None, :]
    gain_key = gain_key[None, :]
    q_r, k_r, v_r, o_all, lse = attend(
        linear, q_inv, k_inv, gain_query, gain_key, cosine, sine, ids, heads
    )
    branch = nn(o_all, w_o).reshape(micro, 4, tok, width)
    branch = scatter_shard([branch[:, j] for j in range(4)])
    hidden = tokens.astype(f32) + branch
    h_scale = inverse_rms(hidden)
    h_n = hidden * h_scale
    b_own = (h_n * gain_mixture).astype(bf16)

    def gather_pair(own):
        got = lax.all_gather(own, "expert", axis=0, tiled=True).reshape(owners, tok, width)
        return got

    def with_near(got):
        return jnp.concatenate([got, swap_core(got)], axis=1)

    do_first = gather_pair(cotangent[0])
    b_own, do_first = tie(b_own, do_first)
    b_got = [gather_pair(b_own[0]), gather_pair(b_own[1])]
    b_first, down_w, second = tie(b_got[0], down_w, cotangent[1])
    b_got[0] = b_first
    do_got = [do_first, gather_pair(second)]
    out_parts = []
    db_list = []
    kept = []
    router_part = jnp.zeros((width, experts), f32)
    for m in range(micro):
        b_now, do_now = b_got[m], do_got[m]
        if m > 0:
            b_now, do_now, _ = tie(b_now, do_now, db_half)
        b_pair = with_near(b_now)
        do_pair = with_near(do_now)
        pick = chosen[m]
        x_p = jnp.einsum("ert,etd->erd", pick, b_pair, preferred_element_type=f32)
        x_p = x_p.astype(bf16).reshape(owners * pack, width)
        b_flat = b_pair.reshape(owners * 2 * tok, width)
        logits = nn(b_flat, router_all)
        pi = jax.nn.softmax(logits, axis=-1)
        is_mine = (jnp.arange(experts) == my_expert).astype(f32)[None, :]
        gate = jnp.sum(pi * is_mine, axis=1)
        gate_p = jnp.einsum(
            "ert,et->er", chosen[m].astype(f32), gate.reshape(owners, 2 * tok), precision=lax.Precision.HIGHEST
        ).reshape(-1, 1)
        gl = nn(x_p, gate_w)
        ul = nn(x_p, up_w)
        sg = 1.0 / (1.0 + jnp.exp(-gl))
        silu = gl * sg
        act = (silu * ul).astype(bf16)
        y = nn(act, down_w).astype(bf16).astype(f32)
        weighted = (gate_p * y).astype(bf16).reshape(owners, pack, width)
        out_part = jnp.einsum("ert,erd->etd", pick, weighted, preferred_element_type=f32).astype(bf16)
        out_half = out_part[:, :tok].astype(f32) + swap_core(out_part[:, tok:]).astype(f32)
        out_parts.append(out_half.astype(bf16))
        do_p = jnp.einsum("ert,etd->erd", pick, do_pair, preferred_element_type=f32)
        do_p = do_p.reshape(owners * pack, width)
        dgate_p = jnp.sum(y * do_p, axis=1)
        dy = (gate_p * do_p).astype(bf16)
        dact = nt(dy, down_w)
        dgl = (dact * ul * sg * (1.0 + gl * (1.0 - sg))).astype(bf16)
        dul = (dact * silu).astype(bf16)
        drow = (nt(dgl, gate_w) + nt(dul, up_w)).astype(bf16).reshape(owners, pack, width)
        dgate = jnp.einsum(
            "ert,er->et", chosen[m].astype(f32), dgate_p.reshape(owners, pack), precision=lax.Precision.HIGHEST
        ).reshape(-1, 1)
        dz = (dgate * gate[:, None] * (is_mine - pi)).astype(bf16)
        router_part = router_part + tn(b_flat, dz)
        db_part = jnp.einsum("ert,erd->etd", pick, drow, preferred_element_type=f32)
        db_part = db_part + nt(dz, router_all).reshape(owners, 2 * tok, width)
        db_half = (db_part[:, :tok] + swap_core(db_part[:, tok:].astype(bf16)).astype(f32)).astype(bf16)
        db_list.append(lax.psum_scatter(db_half, "expert", scatter_dimension=0, tiled=True)[0])
        kept.append((x_p, act, dy, dgl, dul))
    x_k, act_k, dy_k, dgl_k, dul_k = [jnp.concatenate(group, axis=0) for group in zip(*kept)]
    full_gate = tn(x_k, dgl_k)
    full_up = tn(x_k, dul_k)
    full_down = tn(act_k, dy_k)
    mixture_part = jnp.zeros((width,), f32)
    attention_part = jnp.zeros((width,), f32)
    query_part = jnp.zeros((cols,), f32)
    key_part = jnp.zeros((cols,), f32)
    x_own = tokens.astype(f32)
    own_scale = inverse_rms(x_own)
    dh_rows = []
    dqkv_rows = []
    input_grads = []
    for m in range(micro):
        rows_m = slice(m * length, (m + 1) * length)
        db = db_list[m].astype(f32)
        mixture_part = mixture_part + jnp.sum(db * h_n[m], axis=0)
        w_g = db * gain_mixture
        d_hidden = cotangent[m].astype(f32) + h_scale[m] * (
            w_g - h_n[m] * jnp.mean(w_g * h_n[m], axis=-1, keepdims=True)
        )
        dh_m = jnp.concatenate(gather_shard(d_hidden.astype(bf16)), axis=0)
        dh_m, full_gate, full_up, full_down = tie(dh_m, full_gate, full_up, full_down)
        if m > 0:
            sent = [send_side(full, side) for full in (full_gate, full_up, full_down)]
        dh_rows.append(dh_m)
        w_q, w_k, d_v, part_q, part_k, sums = attend_back(
            m, dh_m, w_o, linear, q_r, k_r, v_r, lse, q_inv, k_inv, gain_query, gain_key, cosine, sine, ids, heads
        )
        query_part = query_part + part_q[0]
        key_part = key_part + part_k[0]
        sums = sum_rows(sums[:, 0], core, side, tok) / width
        d_qkv = project_back(m, w_q, w_k, d_v, linear, q_inv, k_inv, sums[0][:, None], sums[1][:, None])
        if m + 1 < micro:
            db_list[m + 1], d_qkv, *out_parts = tie(db_list[m + 1], d_qkv, *out_parts)
            out_own = lax.psum_scatter(jnp.stack(out_parts), "expert", scatter_dimension=1, tiled=True)
        dqkv_rows.append(d_qkv)
        da_part = nt(d_qkv, w_qkv)
        attention_part = attention_part + jnp.sum(da_part * (x_all * x_scale)[rows_m], axis=0)
        da_part = da_part.reshape(4, tok, width)
        da = scatter_shard([da_part[j] for j in range(4)])
        x_n = x_own[m] * own_scale[m]
        a_g = da * gain_attention
        grad = d_hidden + own_scale[m] * (a_g - x_n * jnp.mean(a_g * x_n, axis=-1, keepdims=True))
        input_grads.append(grad.astype(bf16))
    input_grad = jnp.stack(input_grads)
    dh_all = jnp.concatenate(dh_rows, axis=0)
    d_qkv = jnp.concatenate(dqkv_rows, axis=0)
    grad_wo = tn(o_all, dh_all).astype(bf16)
    grad_wo = grad_wo.reshape(owners, rows, 4, cols).transpose(0, 2, 1, 3).reshape(width, cols)

    blank = jnp.zeros((width,), f32)
    gains = jnp.stack(
        [
            attention_part,
            lax.dynamic_update_slice(blank, query_part, (s_index * cols,)),
            lax.dynamic_update_slice(blank, key_part, (s_index * cols,)),
            mixture_part,
        ],
        axis=1,
    )
    (aux_grad,) = tie(
        jnp.concatenate([gains, router_part, jnp.zeros((width, aux_cols - 4 - experts), f32)], axis=1).astype(bf16)
    )
    grad_payload = jnp.concatenate([tn(a_all, d_qkv).astype(bf16), grad_wo, aux_grad], axis=1)
    grad_payload, out_own = tie(grad_payload, out_own)
    output = (hidden + out_own[:, 0].astype(f32)).astype(bf16)
    grad_gate = share_expert_grad(full_gate, sent[0], core, side)
    grad_up = share_expert_grad(full_up, sent[1], core, side)
    grad_down = share_expert_grad(full_down, sent[2], core, side)
    grad_own = lax.psum_scatter(grad_payload, "expert", scatter_dimension=0, tiled=True)
    grad_own = grad_own.reshape(4, rows, 4 * cols + aux_cols)
    grad_wo = grad_own[:, :, 3 * cols : 4 * cols].transpose(1, 0, 2).reshape(rows, width)
    grad_wo = lax.ppermute(grad_wo, BOTH, [(d, b) for b, d in moves]).astype(f32)
    grad_own = jnp.concatenate([grad_own[:, :, : 3 * cols], grad_own[:, :, 4 * cols :]], axis=2)
    grad_own = lax.all_to_all(grad_own, "shard", split_axis=0, concat_axis=0, tiled=True).astype(f32)
    grad_q, grad_k, grad_v = [
        grad_own[:, :, i * cols : (i + 1) * cols].transpose(1, 0, 2).reshape(rows, width)
        for i in range(3)
    ]
    aux_sum = jnp.sum(grad_own[:, :, 3 * cols :], axis=0)
    return (
        output,
        input_grad,
        grad_q,
        grad_k,
        grad_v,
        grad_wo,
        aux_sum[:, 4 : 4 + experts],
        aux_sum[:, 0],
        aux_sum[:, 1],
        aux_sum[:, 2],
        aux_sum[:, 3],
        grad_gate,
        grad_up,
        grad_down,
    )


def solution(mesh):
    tokens_spec = P(None, BOTH, None)
    rows_spec = P(BOTH, None)
    gain_spec = P(BOTH)
    expert_spec = P("expert", "shard", None)
    return jax.shard_map(
        local,
        mesh=mesh,
        in_specs=(tokens_spec, tokens_spec, P(None, "expert", None), tokens_spec)
        + (rows_spec,) * 5
        + (gain_spec,) * 4
        + (expert_spec,) * 3,
        out_specs=(tokens_spec, tokens_spec)
        + (rows_spec,) * 5
        + (gain_spec,) * 4
        + (expert_spec,) * 3,
        check_vma=False,
    )
```

```python
import jax
import jax.numpy as jnp
from jax import lax
from jax.experimental import pallas as pl
from jax.experimental.pallas import tpu as pltpu
from jax.sharding import PartitionSpec as P

HEADS = 16
HEAD_DIM = 128
EPSILON = 1e-05
ROPE_BASE = 10000.0
MASKED = -1e30
BOTH = ("expert", "shard")

f32 = jnp.float32
bf16 = jnp.bfloat16


def dot(left, right, dims):
    return lax.dot_general(left, right, (dims, ((), ())), preferred_element_type=f32)


def nn(left, right):
    return dot(left, right, ((1,), (0,)))


def nt(left, right):
    return dot(left, right, ((1,), (1,)))


def tn(left, right):
    return dot(left, right, ((0,), (0,)))


def swap_core(values):
    return lax.ppermute(values, "shard", [(s, s ^ 1) for s in range(4)])


def swap_side(values):
    return lax.ppermute(values, "shard", [(s, s ^ 2) for s in range(4)])


def gather_shard(values):
    near = swap_core(values)
    far = swap_side(values)
    return [values, near, far, swap_core(far)]


def scatter_shard(parts):
    near = swap_core(jnp.stack([parts[1], parts[3]]).astype(bf16)).astype(f32)
    far = swap_side((parts[2] + near[1]).astype(bf16)).astype(f32)
    return parts[0] + near[0] + far


def tie(*values):
    return lax.optimization_barrier(values)


def low_groups():
    count = lax.axis_size("expert")
    return [[2 * h + low for h in range(count // 2)] for low in range(2)]


def swap_low(values):
    count = lax.axis_size("expert")
    return lax.ppermute(values, "expert", [(e, e ^ 1) for e in range(count)])


def sum_rows(values, core, side, tok):
    def reorder(v):
        v = v.reshape(2, -1, 2, 2, tok)
        v = jnp.where(core == 1, jnp.concatenate([v[:, :, :, 1:], v[:, :, :, :1]], axis=3), v)
        v = jnp.where(side == 1, jnp.concatenate([v[:, :, 1:], v[:, :, :1]], axis=2), v)
        return v.reshape(values.shape)

    return reorder(jnp.sum(lax.all_gather(reorder(values), "shard", axis=0), axis=0))


def inverse_rms(values):
    return lax.rsqrt(jnp.mean(values * values, axis=-1, keepdims=True) + EPSILON)


def attend_body(q_ref, k_ref, v_ref, qi_ref, ki_ref, gq_ref, gk_ref, cos_ref, sin_ref, idq_ref, idk_ref,
                qr_ref, kr_ref, vr_ref, o_ref, lse_ref):
    cos = cos_ref[...]
    sin = sin_ref[...]
    half = HEAD_DIM // 2

    def rope(values):
        return (values * cos + pltpu.roll(values, half, 1) * sin).astype(bf16)

    q_r = rope(q_ref[...] * qi_ref[...] * gq_ref[...])
    k_r = rope(k_ref[...] * ki_ref[...] * gk_ref[...])
    v_r = v_ref[...].astype(bf16)
    qr_ref[...] = q_r
    kr_ref[...] = k_r
    vr_ref[...] = v_r
    scores = jnp.where(idk_ref[0] <= idq_ref[...], nt(q_r, k_r) * HEAD_DIM ** (-0.5), MASKED)
    peak = jnp.max(scores, axis=-1, keepdims=True)
    weight = jnp.exp(scores - peak)
    total = jnp.sum(weight, axis=-1, keepdims=True)
    o_ref[...] = nn((weight / total).astype(bf16), v_r).astype(bf16)
    lse_ref[0] = peak + jnp.log(total)


def attend(linear, q_inv, k_inv, gain_q, gain_k, cos, sin, ids, heads):
    micro, length = ids.shape
    cols = heads * HEAD_DIM
    total = micro * length
    head = lambda base: pl.BlockSpec((length, HEAD_DIM), lambda m, h: (m, base + h))
    column = pl.BlockSpec((length, 1), lambda m, h: (m, 0))
    gain = pl.BlockSpec((1, HEAD_DIM), lambda m, h: (0, h))
    angle = pl.BlockSpec((length, HEAD_DIM), lambda m, h: (0, 0))
    keys = pl.BlockSpec((1, 1, length), lambda m, h: (m, 0, 0))
    low = jax.ShapeDtypeStruct((total, cols), bf16)
    return pl.pallas_call(
        attend_body,
        grid=(micro, heads),
        in_specs=[head(0), head(heads), head(2 * heads), column, column, gain, gain, angle, angle, column, keys],
        out_specs=[head(0)] * 4 + [pl.BlockSpec((1, length, 1), lambda m, h: (m * heads + h, 0, 0))],
        out_shape=[low] * 4 + [jax.ShapeDtypeStruct((micro * heads, length, 1), f32)],
    )(linear, linear, linear, q_inv, k_inv, gain_q, gain_k, cos, sin, ids.reshape(total, 1), ids[:, None, :])


def exact(left, right, at):
    dims = (((1,), (at,)), ((), ()))
    return lax.dot_general(left, right, dims, precision=lax.Precision.HIGHEST, preferred_element_type=f32)


def attend_back_body(dh_ref, wo_ref, q_ref, k_ref, qr_ref, kr_ref, vr_ref, lse_ref, qi_ref, ki_ref, gq_ref, gk_ref,
                     cos_ref, sin_ref, idq_ref, idk_ref, order_ref, wq_ref, wk_ref, dv_ref, pq_ref, pk_ref, sum_ref):
    cos = cos_ref[...]
    sin = sin_ref[...]
    half = HEAD_DIM // 2
    scale = HEAD_DIM ** (-0.5)
    q_r = qr_ref[...]
    k_r = kr_ref[...]
    d_o = nt(dh_ref[...], wo_ref[...]).astype(bf16)
    scores = jnp.where(idk_ref[0] <= idq_ref[...], nt(q_r, k_r) * scale, MASKED)
    prob = jnp.exp(scores - lse_ref[0])
    d_prob = nt(d_o, vr_ref[...])
    delta = jnp.sum(prob * d_prob, axis=-1, keepdims=True)
    d_s = (prob * (d_prob - delta)).astype(bf16)
    dv_ref[...] = tn(prob.astype(bf16), d_o).astype(bf16)
    ones = jnp.ones((8, HEAD_DIM), f32)

    def finish(grad, linear, inverse, gain, out_ref, part_ref, at):
        grad = grad * scale
        grad = grad * cos - pltpu.roll(grad, half, 1) * sin
        normed = linear * inverse
        part_ref[...] = jnp.sum(grad * normed, axis=0, keepdims=True)
        grad = grad * gain
        out_ref[...] = grad
        rows = exact(ones, grad * normed, 1)

        rows = exact(rows, order_ref[...], 0)[:1]

        @pl.when(pl.program_id(0) == 0)
        def _():
            sum_ref[at : at + 1] = rows

        @pl.when(pl.program_id(0) > 0)
        def _():
            sum_ref[at : at + 1] = sum_ref[at : at + 1] + rows

    finish(nn(d_s, k_r), q_ref[...], qi_ref[...], gq_ref[...], wq_ref, pq_ref, 0)
    finish(tn(d_s, q_r), k_ref[...], ki_ref[...], gk_ref[...], wk_ref, pk_ref, 1)


def attend_back(m, dh, w_o, linear, q_r, k_r, v_r, lse, q_inv, k_inv, gain_q, gain_k, cos, sin, ids, order, heads):
    micro, length = ids.shape
    cols = heads * HEAD_DIM
    width = dh.shape[1]
    head = lambda base: pl.BlockSpec((length, HEAD_DIM), lambda h: (m, base + h))
    column = pl.BlockSpec((length, 1), lambda h: (m, 0))
    gain = pl.BlockSpec((1, HEAD_DIM), lambda h: (0, h))
    angle = pl.BlockSpec((length, HEAD_DIM), lambda h: (0, 0))
    keys = pl.BlockSpec((1, 1, length), lambda h: (m, 0, 0))
    out = pl.BlockSpec((length, HEAD_DIM), lambda h: (0, h))
    return pl.pallas_call(
        attend_back_body,
        grid=(heads,),
        in_specs=[
            pl.BlockSpec((length, width), lambda h: (0, 0)),
            pl.BlockSpec((HEAD_DIM, width), lambda h: (h, 0)),
            head(0), head(heads), head(0), head(0), head(0),
            pl.BlockSpec((1, length, 1), lambda h: (m * heads + h, 0, 0)),
            column, column, gain, gain, angle, angle, column, keys,
            pl.BlockSpec((length, length), lambda h: (0, 0)),
        ],
        out_specs=[out, out, out, gain, gain, pl.BlockSpec((2, length), lambda h: (0, 0))],
        out_shape=[
            jax.ShapeDtypeStruct((length, cols), f32),
            jax.ShapeDtypeStruct((length, cols), f32),
            jax.ShapeDtypeStruct((length, cols), bf16),
            jax.ShapeDtypeStruct((1, cols), f32),
            jax.ShapeDtypeStruct((1, cols), f32),
            jax.ShapeDtypeStruct((2, length), f32),
        ],
    )(dh, w_o, linear, linear, q_r, k_r, v_r, lse, q_inv, k_inv, gain_q, gain_k, cos, sin,
      ids.reshape(micro * length, 1), ids[:, None, :], order)


def project_back_body(wq_ref, wk_ref, dv_ref, q_ref, k_ref, qi_ref, ki_ref, sum_ref, order_ref, out_ref):
    cols = wq_ref.shape[1]
    q_inv = qi_ref[...]
    k_inv = ki_ref[...]
    total = sum_ref[0] + sum_ref[1] + sum_ref[2] + sum_ref[3]
    total = exact(order_ref[...], total, 1) * (1.0 / (4 * cols))
    out_ref[:, :cols] = (q_inv * (wq_ref[...] - q_ref[...] * (q_inv * total[:, :1]))).astype(bf16)
    out_ref[:, cols : 2 * cols] = (k_inv * (wk_ref[...] - k_ref[...] * (k_inv * total[:, 1:]))).astype(bf16)
    out_ref[:, 2 * cols :] = dv_ref[...]


def project_back(m, w_q, w_k, d_v, linear, q_inv, k_inv, sums, order):
    length, cols = w_q.shape
    rows = length // 2
    full = pl.BlockSpec((rows, cols), lambda i: (i, 0))
    column = pl.BlockSpec((rows, 1), lambda i: (2 * m + i, 0))
    return pl.pallas_call(
        project_back_body,
        grid=(2,),
        in_specs=[full, full, full]
        + [pl.BlockSpec((rows, cols), lambda i, b=b: (2 * m + i, b)) for b in range(2)]
        + [column, column, pl.BlockSpec(sums.shape, lambda i: (0, 0, 0)), pl.BlockSpec((rows, length), lambda i: (i, 0))],
        out_specs=pl.BlockSpec((rows, 3 * cols), lambda i: (i, 0)),
        out_shape=jax.ShapeDtypeStruct((length, 3 * cols), bf16),
    )(w_q, w_k, d_v, linear, linear, q_inv, k_inv, sums, order)


def expert_body(slot_ref, bo_ref, bn_ref, do_ref, dn_ref, wg_ref, wu_ref, wd_ref, router_ref, mine_ref,
                x_ref, act_ref, dy_ref, dgl_ref, dul_ref, oo_ref, on_ref, go_ref, gn_ref, part_ref):
    group = slot_ref.shape[0]
    pack = x_ref.shape[1]
    tok, width = bo_ref.shape[-2:]
    router = router_ref[...]
    mine = mine_ref[...]
    picks, gates, xs, dos, pis, bs = [], [], [], [], [], []
    for g in range(group):
        both = lambda own, near: jnp.concatenate([own[g].reshape(tok, width), near[g].reshape(tok, width)], axis=0)
        b = both(bo_ref, bn_ref)
        logits = nt(router, b)
        weight = jnp.exp(logits - jnp.max(logits, axis=0, keepdims=True))
        pi = weight / jnp.sum(weight, axis=0, keepdims=True)
        slots = lax.broadcasted_iota(jnp.int32, (pack, 2 * tok), 0)
        pick = jnp.where(slots == slot_ref[g], 1.0, 0.0)
        gate = jnp.sum(pi * mine, axis=0, keepdims=True)
        gates.append((gate, jnp.sum(pick * gate, axis=1, keepdims=True)))
        low = pick.astype(bf16)
        picks.append((pick, low))
        xs.append(nn(low, b).astype(bf16))
        dos.append(nn(low, both(do_ref, dn_ref)))
        pis.append(pi)
        bs.append(b)
    x = jnp.concatenate(xs, axis=0)
    gate_p = jnp.concatenate([g[1] for g in gates], axis=0)
    gl = nn(x, wg_ref[...])
    ul = nn(x, wu_ref[...])
    sg = 1.0 / (1.0 + jnp.exp(-gl))
    silu = gl * sg
    act = (silu * ul).astype(bf16)
    do_p = jnp.concatenate(dos, axis=0)
    dy = (gate_p * do_p).astype(bf16)
    y = nn(act, wd_ref[...]).astype(bf16).astype(f32)
    dgate_p = jnp.sum(y * do_p, axis=1, keepdims=True)
    weighted = (gate_p * y).astype(bf16)
    dact = nt(dy, wd_ref[...])
    dgl = (dact * ul * sg * (1.0 + gl * (1.0 - sg))).astype(bf16)
    dul = (dact * silu).astype(bf16)
    drow = (nt(dgl, wg_ref[...]) + nt(dul, wu_ref[...])).astype(bf16)
    total = None
    for g in range(group):
        rows = slice(g * pack, (g + 1) * pack)
        pick, low = picks[g]
        x_ref[g] = x[rows]
        act_ref[g] = act[rows]
        dy_ref[g] = dy[rows]
        dgl_ref[g] = dgl[rows]
        dul_ref[g] = dul[rows]
        out = tn(low, weighted[rows]).astype(bf16)
        oo_ref[g] = out[:tok]
        on_ref[g] = out[tok:]
        dgate = jnp.sum(pick * dgate_p[rows], axis=0, keepdims=True)
        dz = (dgate * gates[g][0] * (mine - pis[g])).astype(bf16)
        grad = (tn(low, drow[rows]) + tn(dz, router)).astype(bf16)
        go_ref[g] = grad[:tok]
        gn_ref[g] = grad[tok:]
        part = nn(dz, bs[g])
        total = part if total is None else total + part

    @pl.when(pl.program_id(0) == 0)
    def _():
        part_ref[...] = total

    @pl.when(pl.program_id(0) > 0)
    def _():
        part_ref[...] = part_ref[...] + total


def expert_step(slot, b_own, b_near, do_own, do_near, gate_w, up_w, down_w, router_t, mine, pack):
    group = 2
    owners = slot.shape[0]
    width, hidden = gate_w.shape
    tok = slot.shape[2] // 2
    experts = router_t.shape[0]

    def rows_spec(value):
        if isinstance(value, tuple):
            at = value[1]
            return pl.BlockSpec((group, 1, tok, width), lambda i: (i, at, 0, 0))
        return pl.BlockSpec((group, tok, width), lambda i: (i, 0, 0))

    def fixed(shape):
        return pl.BlockSpec(shape, lambda i: (0, 0), pipeline_mode=pl.Buffered(1))

    def packed(cols):
        return pl.BlockSpec((group, pack, cols), lambda i: (i, 0, 0))

    token = pl.BlockSpec((group, tok, width), lambda i: (i, 0, 0))
    values = (b_own, b_near, do_own, do_near)
    widths = (width, hidden, width, hidden, hidden)
    return pl.pallas_call(
        expert_body,
        grid=(owners // group,),
        in_specs=[pl.BlockSpec((group, 1, 2 * tok), lambda i: (i, 0, 0))]
        + [rows_spec(v) for v in values]
        + [fixed(gate_w.shape), fixed(up_w.shape), fixed(down_w.shape), fixed(router_t.shape), fixed(mine.shape)],
        out_specs=[packed(c) for c in widths] + [token] * 4 + [pl.BlockSpec((experts, width), lambda i: (0, 0))],
        out_shape=[jax.ShapeDtypeStruct((owners, pack, c), bf16) for c in widths]
        + [jax.ShapeDtypeStruct((owners, tok, width), bf16)] * 4
        + [jax.ShapeDtypeStruct((experts, width), f32)],
        compiler_params=pltpu.CompilerParams(vmem_limit_bytes=60 * 1024 * 1024),
    )(slot, *[v[0] if isinstance(v, tuple) else v for v in values], gate_w, up_w, down_w, router_t, mine)


def half_expert(weight, core):
    other = lax.dynamic_index_in_dim(weight, 1 - core, 0, keepdims=True)
    return lax.dynamic_update_slice(weight, swap_core(other), (1 - core, 0, 0))


def whole_expert(half, side):
    far = swap_side(half)
    whole = jnp.concatenate([half, half], axis=0)
    whole = lax.dynamic_update_slice(whole, far, (2 * (1 - side), 0, 0))
    return whole.reshape(4 * half.shape[1], half.shape[2])


def send_side(grad, side):
    grad = grad.reshape(4, grad.shape[0] // 4, grad.shape[1])
    return swap_side(lax.dynamic_slice_in_dim(grad, 2 * (1 - side), 2, 0).astype(bf16))


def share_expert_grad(grad, far, core, side):
    grad = grad.reshape(4, grad.shape[0] // 4, grad.shape[1])
    mine = lax.dynamic_slice_in_dim(grad, 2 * side, 2, 0) + far.astype(f32)
    near = swap_core(lax.dynamic_index_in_dim(mine, 1 - core, 0, keepdims=True).astype(bf16))
    return lax.dynamic_update_slice(mine, near.astype(f32), (1 - core, 0, 0))


def local(
    tokens,
    cotangent,
    block_ids,
    routes,
    w_query,
    w_key,
    w_value,
    w_out,
    router,
    attention_gain,
    query_gain,
    key_gain,
    mixture_gain,
    w_gate,
    w_up,
    w_down,
):
    micro, tok, width = tokens.shape
    owners = lax.axis_size("expert")
    experts = router.shape[1]
    capacity = (tok * routes.shape[2] * 9 + 8 * experts - 1) // (8 * experts)
    pack = (2 * capacity + 15) // 16 * 16
    rows = w_query.shape[0]
    cols = width // 4
    heads = HEADS // 4
    length = 4 * tok
    s_index = lax.axis_index("shard")
    e_index = lax.axis_index("expert")
    core = s_index % 2
    side = s_index // 2
    my_expert = 2 * e_index + core

    top = routes.shape[2]
    route_cols = micro * tok * top // rows
    used = 4 + experts + route_cols
    aux_cols = (used + 127) // 128 * 128
    aux = jnp.concatenate(
        [
            jnp.stack([attention_gain, query_gain, key_gain, mixture_gain], axis=1),
            router,
            routes.astype(bf16).transpose(0, 2, 1).reshape(rows, route_cols),
            jnp.zeros((rows, aux_cols - used), bf16),
        ],
        axis=1,
    )
    blocks = [w.reshape(rows, 4, cols) for w in (w_query, w_key, w_value)]
    blocks.append(jnp.broadcast_to(aux[:, None, :], (rows, 4, aux_cols)))
    payload = jnp.concatenate(blocks, axis=2).transpose(1, 0, 2)
    payload = lax.all_to_all(payload, "shard", split_axis=0, concat_axis=0, tiled=True)
    do_got = lax.all_gather(cotangent[0], "expert", axis=0, axis_index_groups=low_groups())
    payload, do_got = tie(payload, do_got)
    front = lax.all_gather(payload.reshape(4 * rows, 3 * cols + aux_cols), "expert", axis=0, tiled=True)

    gate_w = whole_expert(half_expert(w_gate, core), side)
    down_w = whole_expert(half_expert(w_down, core), side)
    chunks = gather_shard(tokens)
    devices = 4 * owners
    moves = [(b, (b % owners) * 4 + b // owners) for b in range(devices)]
    w_o_block = lax.ppermute(w_out, BOTH, moves)
    x_all = jnp.concatenate(chunks, axis=1).reshape(micro * length, width)
    x_scale = inverse_rms(x_all.astype(f32))
    chunk_ids = [jnp.bitwise_xor(s_index, j) for j in range(4)]
    positions = jnp.concatenate([c * tok + jnp.arange(tok, dtype=jnp.int32) for c in chunk_ids])
    order = (positions[:, None] == jnp.arange(length)[None, :]).astype(f32)
    rate = ROPE_BASE ** (-2.0 * jnp.arange(HEAD_DIM // 2, dtype=f32) / HEAD_DIM)
    angles = positions.astype(f32)[:, None] * rate[None, :]
    cosine = jnp.cos(angles)
    sine = jnp.sin(angles)
    cosine = jnp.concatenate([cosine, cosine], axis=1)
    sine = jnp.concatenate([-sine, sine], axis=1)
    up_w = whole_expert(half_expert(w_up, core), side)
    front, gate_w, up_w, w_o_block, x_all, x_scale, cosine, sine = tie(
        front, gate_w, up_w, w_o_block, x_all, x_scale, cosine, sine
    )
    do_got, _ = tie(do_got, front)
    do_other = swap_low(do_got)
    w_o = lax.all_gather(w_o_block, "expert", axis=0, tiled=True)
    w_qkv = front[:, : 3 * cols]
    aux_rows = front[:, 3 * cols :].T.astype(f32)
    gain_attention = aux_rows[0]
    gain_query = lax.dynamic_slice_in_dim(aux_rows[1], s_index * cols, cols)
    gain_key = lax.dynamic_slice_in_dim(aux_rows[2], s_index * cols, cols)
    gain_mixture = aux_rows[3]


    all_routes = front[:, 3 * cols + 4 + experts : 3 * cols + used].astype(jnp.int32)
    all_routes = all_routes.reshape(owners, 4, micro, top, tok)
    mine = all_routes == my_expert
    mine = jnp.any(mine, axis=3)
    pair = [lax.dynamic_index_in_dim(mine, s_index ^ j, 1, keepdims=False) for j in range(2)]
    mask = jnp.concatenate(pair, axis=2).transpose(1, 0, 2)
    places = jnp.arange(2 * tok)
    earlier = (places[:, None] < places[None, :]).astype(bf16)
    slot = jnp.einsum("met,tu->meu", mask.astype(bf16), earlier, preferred_element_type=f32)
    slot = jnp.where(mask, slot.astype(jnp.int32), -1)
    slot = slot[:, :, None, :]

    a_all = (x_all.astype(f32) * x_scale * gain_attention).astype(bf16)
    linear = nn(a_all, w_qkv)
    q_lin = linear[:, :cols]
    k_lin = linear[:, cols : 2 * cols]
    sums = jnp.stack([jnp.sum(q_lin * q_lin, axis=1), jnp.sum(k_lin * k_lin, axis=1)])
    sums = sum_rows(sums, core, side, tok)
    inv = lax.rsqrt(sums / width + EPSILON)
    q_inv = inv[0][:, None]
    k_inv = inv[1][:, None]
    ids = block_ids[:, 0, :]
    ids = jnp.concatenate(
        [lax.dynamic_slice_in_dim(ids, c * tok, tok, axis=1) for c in chunk_ids], axis=1
    )
    gain_query = gain_query[None, :]
    gain_key = gain_key[None, :]
    q_r, k_r, v_r, o_all, lse = attend(
        linear, q_inv, k_inv, gain_query, gain_key, cosine, sine, ids, heads
    )
    branch = nn(o_all, w_o).reshape(micro, 4, tok, width)
    branch = scatter_shard([branch[:, j] for j in range(4)])
    hidden = tokens.astype(f32) + branch
    h_scale = inverse_rms(hidden)
    h_n = hidden * h_scale
    b_own = (h_n * gain_mixture).astype(bf16)

    def gather_expert(own):
        return lax.all_gather(own, "expert", axis=0, tiled=True)

    my_expert = 2 * e_index + core
    low = e_index % 2
    do_first = jnp.stack(
        [jnp.where(low == 0, do_got, do_other), jnp.where(low == 0, do_other, do_got)], axis=1
    ).reshape(owners, tok, width)
    b_first = gather_expert(b_own[0][None])
    second = gather_expert(jnp.stack([b_own[1], cotangent[1]])[None])
    b_first, down_w = tie(b_first, down_w)
    out_parts = []
    db_list = []
    kept = []
    router_t = front[:, 3 * cols + 4 : 3 * cols + 4 + experts].T
    is_mine = (jnp.arange(experts) == my_expert).astype(f32)[:, None]
    router_part = jnp.zeros((experts, width), f32)
    for m in range(micro):
        if m == 0:
            values = (b_first, swap_core(b_first), do_first, swap_core(do_first))
        else:
            second, _ = tie(second, db_half)
            near = swap_core(second)
            values = ((second, 0), (near, 0), (second, 1), (near, 1))
        *saved, out_mine, out_near, db_mine, db_near, part = expert_step(
            slot[m], *values, gate_w, up_w, down_w, router_t, is_mine, pack
        )
        router_part = router_part + part
        db_half = (db_mine.astype(f32) + swap_core(db_near).astype(f32)).astype(bf16)
        db_list.append(lax.psum_scatter(db_half, "expert", scatter_dimension=0, tiled=True)[0])
        out_parts.append((out_mine, out_near))
        kept.append([v.reshape(owners * pack, v.shape[2]) for v in saved])
    x_k, act_k, dy_k, dgl_k, dul_k = [jnp.concatenate(group, axis=0) for group in zip(*kept)]
    outs = [v for pair in out_parts for v in pair]
    _, db_list[0], x_k, act_k, *outs = tie(db_half, db_list[0], x_k, act_k, *outs)
    out_parts = [
        (outs[2 * m].astype(f32) + swap_core(outs[2 * m + 1]).astype(f32)).astype(bf16) for m in range(micro)
    ]
    full_gate = tn(x_k, dgl_k)
    full_up = tn(x_k, dul_k)
    full_down = tn(act_k, dy_k)
    mixture_part = jnp.zeros((width,), f32)
    query_part = jnp.zeros((cols,), f32)
    key_part = jnp.zeros((cols,), f32)
    x_own = tokens.astype(f32)
    own_scale = inverse_rms(x_own)
    dh_rows = []
    dqkv_rows = []
    d_hiddens = []
    input_grads = []
    for m in range(micro):
        db = db_list[m].astype(f32)
        mixture_part = mixture_part + jnp.sum(db * h_n[m], axis=0)
        w_g = db * gain_mixture
        d_hidden = cotangent[m].astype(f32) + h_scale[m] * (
            w_g - h_n[m] * jnp.mean(w_g * h_n[m], axis=-1, keepdims=True)
        )
        dh_m = jnp.concatenate(gather_shard(d_hidden.astype(bf16)), axis=0)
        if m == 0:
            out_part = jnp.stack(out_parts, axis=1)
            dh_m, full_gate, full_up, full_down, out_part = tie(dh_m, full_gate, full_up, full_down, out_part)
        dh_rows.append(dh_m)
        w_q, w_k, d_v, part_q, part_k, sums = attend_back(
            m, dh_m, w_o, linear, q_r, k_r, v_r, lse, q_inv, k_inv, gain_query, gain_key, cosine, sine, ids, order, heads
        )
        query_part = query_part + part_q[0]
        key_part = key_part + part_k[0]
        sums = lax.all_gather(sums, "shard", axis=0)
        d_qkv = project_back(m, w_q, w_k, d_v, linear, q_inv, k_inv, sums, order)
        if m + 1 < micro:
            db_list[m + 1], d_qkv, out_part = tie(db_list[m + 1], d_qkv, out_part)
            out_own = lax.psum_scatter(out_part, "expert", scatter_dimension=0, tiled=True)[0]
        dqkv_rows.append(d_qkv)
        d_hiddens.append(d_hidden)
    dh_all = jnp.concatenate(dh_rows, axis=0)
    grad_wo = jnp.stack(
        [tn(o_all, dh_all[:, i * cols : (i + 1) * cols]).astype(bf16).reshape(owners, rows, cols) for i in range(4)],
        axis=1,
    ).reshape(width, cols)

    blank = jnp.zeros((width,), f32)
    gains = jnp.stack(
        [
            blank,
            lax.dynamic_update_slice(blank, query_part, (s_index * cols,)),
            lax.dynamic_update_slice(blank, key_part, (s_index * cols,)),
            mixture_part,
        ],
        axis=1,
    )
    (aux_grad,) = tie(
        jnp.concatenate([gains, router_part.T, jnp.zeros((width, aux_cols - 4 - experts), f32)], axis=1).astype(bf16)
    )
    grad_payload = jnp.concatenate([tn(a_all, jnp.concatenate(dqkv_rows, axis=0)).astype(bf16), grad_wo, aux_grad], axis=1)
    grad_payload, out_own, *dqkv_rows = tie(grad_payload, out_own, *dqkv_rows)
    grad_own = lax.psum_scatter(grad_payload, "expert", scatter_dimension=0, tiled=True)
    output = (hidden + out_own.astype(f32)).astype(bf16)
    for m in range(micro):
        da_part = nt(dqkv_rows[m], w_qkv)
        da_part = da_part.reshape(4, tok, width)
        da = scatter_shard([da_part[j] for j in range(4)])
        da, full_gate, full_up, full_down = tie(da, full_gate, full_up, full_down)
        x_n = x_own[m] * own_scale[m]
        a_g = da * gain_attention
        grad = d_hiddens[m] + own_scale[m] * (a_g - x_n * jnp.mean(a_g * x_n, axis=-1, keepdims=True))
        input_grads.append(grad.astype(bf16))
    input_grad = jnp.stack(input_grads)
    sent_gate = send_side(full_gate, side)
    sent_up = send_side(full_up, side)
    sent_down = send_side(full_down, side)
    grad_gate = share_expert_grad(full_gate, sent_gate, core, side)
    grad_up = share_expert_grad(full_up, sent_up, core, side)
    grad_down = share_expert_grad(full_down, sent_down, core, side)
    grad_own = grad_own.reshape(4, rows, 4 * cols + aux_cols)
    grad_wo = grad_own[:, :, 3 * cols : 4 * cols].transpose(1, 0, 2).reshape(rows, width)
    grad_wo = lax.ppermute(grad_wo, BOTH, [(d, b) for b, d in moves]).astype(f32)
    grad_own = jnp.concatenate([grad_own[:, :, : 3 * cols], grad_own[:, :, 4 * cols :]], axis=2)
    grad_own = lax.all_to_all(grad_own, "shard", split_axis=0, concat_axis=0, tiled=True).astype(f32)
    grad_q, grad_k, grad_v = [
        grad_own[:, :, i * cols : (i + 1) * cols].transpose(1, 0, 2).reshape(rows, width)
        for i in range(3)
    ]
    aux_sum = jnp.sum(grad_own[:, :, 3 * cols :], axis=0)
    grad_gain = sum(
        jnp.sum(w.astype(f32) * g, axis=1) for w, g in ((w_query, grad_q), (w_key, grad_k), (w_value, grad_v))
    )
    grad_gain = grad_gain / attention_gain.astype(f32)
    return (
        output,
        input_grad,
        grad_q,
        grad_k,
        grad_v,
        grad_wo,
        aux_sum[:, 4 : 4 + experts],
        grad_gain,
        aux_sum[:, 1],
        aux_sum[:, 2],
        aux_sum[:, 3],
        grad_gate,
        grad_up,
        grad_down,
    )


def solution(mesh):
    tokens_spec = P(None, BOTH, None)
    rows_spec = P(BOTH, None)
    gain_spec = P(BOTH)
    expert_spec = P("expert", "shard", None)
    return jax.shard_map(
        local,
        mesh=mesh,
        in_specs=(tokens_spec, tokens_spec, P(None, "expert", None), tokens_spec)
        + (rows_spec,) * 5
        + (gain_spec,) * 4
        + (expert_spec,) * 3,
        out_specs=(tokens_spec, tokens_spec)
        + (rows_spec,) * 5
        + (gain_spec,) * 4
        + (expert_spec,) * 3,
        check_vma=False,
    )
```

```python
import jax
import jax.numpy as jnp
from jax import lax
from jax.experimental import pallas as pl
from jax.experimental.pallas import tpu as pltpu
from jax.sharding import PartitionSpec as P

HEADS = 16
HEAD_DIM = 128
EPSILON = 1e-05
ROPE_BASE = 10000.0
MASKED = -1e30
BOTH = ("expert", "shard")

f32 = jnp.float32
bf16 = jnp.bfloat16


def dot(left, right, dims):
    return lax.dot_general(left, right, (dims, ((), ())), preferred_element_type=f32)


def nn(left, right):
    return dot(left, right, ((1,), (0,)))


def nt(left, right):
    return dot(left, right, ((1,), (1,)))


def tn(left, right):
    return dot(left, right, ((0,), (0,)))


def swap_core(values):
    return lax.ppermute(values, "shard", [(s, s ^ 1) for s in range(4)])


def swap_side(values):
    return lax.ppermute(values, "shard", [(s, s ^ 2) for s in range(4)])


def gather_shard(values):
    near = swap_core(values)
    far = swap_side(values)
    return [values, near, far, swap_core(far)]


def scatter_shard(parts):
    near = swap_core(jnp.stack([parts[1], parts[3]]).astype(bf16)).astype(f32)
    far = swap_side((parts[2] + near[1]).astype(bf16)).astype(f32)
    return parts[0] + near[0] + far


def tie(*values):
    return lax.optimization_barrier(values)


def low_groups():
    count = lax.axis_size("expert")
    return [[2 * h + low for h in range(count // 2)] for low in range(2)]


def swap_low(values):
    count = lax.axis_size("expert")
    return lax.ppermute(values, "expert", [(e, e ^ 1) for e in range(count)])


def sum_rows(values, core, side, tok):
    def reorder(v):
        v = v.reshape(2, -1, 2, 2, tok)
        v = jnp.where(core == 1, jnp.concatenate([v[:, :, :, 1:], v[:, :, :, :1]], axis=3), v)
        v = jnp.where(side == 1, jnp.concatenate([v[:, :, 1:], v[:, :, :1]], axis=2), v)
        return v.reshape(values.shape)

    return reorder(jnp.sum(lax.all_gather(reorder(values), "shard", axis=0), axis=0))


def inverse_rms(values):
    return lax.rsqrt(jnp.mean(values * values, axis=-1, keepdims=True) + EPSILON)


def attend_body(q_ref, k_ref, v_ref, qi_ref, ki_ref, gq_ref, gk_ref, cos_ref, sin_ref, idq_ref, idk_ref,
                qr_ref, kr_ref, vr_ref, o_ref, lse_ref):
    cos = cos_ref[...]
    sin = sin_ref[...]
    half = HEAD_DIM // 2

    def rope(values):
        return (values * cos + pltpu.roll(values, half, 1) * sin).astype(bf16)

    q_r = rope(q_ref[...] * qi_ref[...] * gq_ref[...])
    k_r = rope(k_ref[...] * ki_ref[...] * gk_ref[...])
    v_r = v_ref[...].astype(bf16)
    qr_ref[...] = q_r
    kr_ref[...] = k_r
    vr_ref[...] = v_r
    scores = jnp.where(idk_ref[0] <= idq_ref[...], nt(q_r, k_r) * HEAD_DIM ** (-0.5), MASKED)
    peak = jnp.max(scores, axis=-1, keepdims=True)
    weight = jnp.exp(scores - peak)
    total = jnp.sum(weight, axis=-1, keepdims=True)
    o_ref[...] = nn((weight / total).astype(bf16), v_r).astype(bf16)
    lse_ref[0] = peak + jnp.log(total)


def attend(linear, q_inv, k_inv, gain_q, gain_k, cos, sin, ids, heads):
    micro, length = ids.shape
    cols = heads * HEAD_DIM
    total = micro * length
    head = lambda base: pl.BlockSpec((length, HEAD_DIM), lambda m, h: (m, base + h))
    column = pl.BlockSpec((length, 1), lambda m, h: (m, 0))
    gain = pl.BlockSpec((1, HEAD_DIM), lambda m, h: (0, h))
    angle = pl.BlockSpec((length, HEAD_DIM), lambda m, h: (0, 0))
    keys = pl.BlockSpec((1, 1, length), lambda m, h: (m, 0, 0))
    low = jax.ShapeDtypeStruct((total, cols), bf16)
    return pl.pallas_call(
        attend_body,
        grid=(micro, heads),
        in_specs=[head(0), head(heads), head(2 * heads), column, column, gain, gain, angle, angle, column, keys],
        out_specs=[head(0)] * 4 + [pl.BlockSpec((1, length, 1), lambda m, h: (m * heads + h, 0, 0))],
        out_shape=[low] * 4 + [jax.ShapeDtypeStruct((micro * heads, length, 1), f32)],
    )(linear, linear, linear, q_inv, k_inv, gain_q, gain_k, cos, sin, ids.reshape(total, 1), ids[:, None, :])


def exact(left, right, at):
    dims = (((1,), (at,)), ((), ()))
    return lax.dot_general(left, right, dims, precision=lax.Precision.HIGHEST, preferred_element_type=f32)


def attend_back_body(dh_ref, wo_ref, q_ref, k_ref, qr_ref, kr_ref, vr_ref, lse_ref, qi_ref, ki_ref, gq_ref, gk_ref,
                     cos_ref, sin_ref, idq_ref, idk_ref, order_ref, wq_ref, wk_ref, dv_ref, pq_ref, pk_ref, sum_ref):
    cos = cos_ref[...]
    sin = sin_ref[...]
    half = HEAD_DIM // 2
    scale = HEAD_DIM ** (-0.5)
    q_r = qr_ref[...]
    k_r = kr_ref[...]
    d_o = nt(dh_ref[...], wo_ref[...]).astype(bf16)
    scores = jnp.where(idk_ref[0] <= idq_ref[...], nt(q_r, k_r) * scale, MASKED)
    prob = jnp.exp(scores - lse_ref[0])
    d_prob = nt(d_o, vr_ref[...])
    delta = jnp.sum(prob * d_prob, axis=-1, keepdims=True)
    d_s = (prob * (d_prob - delta)).astype(bf16)
    dv_ref[...] = tn(prob.astype(bf16), d_o).astype(bf16)
    ones = jnp.ones((8, HEAD_DIM), f32)

    def finish(grad, linear, inverse, gain, out_ref, part_ref, at):
        grad = grad * scale
        grad = grad * cos - pltpu.roll(grad, half, 1) * sin
        normed = linear * inverse
        part_ref[...] = jnp.sum(grad * normed, axis=0, keepdims=True)
        grad = grad * gain
        out_ref[...] = grad
        rows = exact(ones, grad * normed, 1)

        rows = exact(rows, order_ref[...], 0)[:1]

        @pl.when(pl.program_id(0) == 0)
        def _():
            sum_ref[at : at + 1] = rows

        @pl.when(pl.program_id(0) > 0)
        def _():
            sum_ref[at : at + 1] = sum_ref[at : at + 1] + rows

    finish(nn(d_s, k_r), q_ref[...], qi_ref[...], gq_ref[...], wq_ref, pq_ref, 0)
    finish(tn(d_s, q_r), k_ref[...], ki_ref[...], gk_ref[...], wk_ref, pk_ref, 1)


def attend_back(m, dh, w_o, linear, q_r, k_r, v_r, lse, q_inv, k_inv, gain_q, gain_k, cos, sin, ids, order, heads):
    micro, length = ids.shape
    cols = heads * HEAD_DIM
    width = dh.shape[1]
    head = lambda base: pl.BlockSpec((length, HEAD_DIM), lambda h: (m, base + h))
    column = pl.BlockSpec((length, 1), lambda h: (m, 0))
    gain = pl.BlockSpec((1, HEAD_DIM), lambda h: (0, h))
    angle = pl.BlockSpec((length, HEAD_DIM), lambda h: (0, 0))
    keys = pl.BlockSpec((1, 1, length), lambda h: (m, 0, 0))
    out = pl.BlockSpec((length, HEAD_DIM), lambda h: (0, h))
    return pl.pallas_call(
        attend_back_body,
        grid=(heads,),
        in_specs=[
            pl.BlockSpec((length, width), lambda h: (0, 0)),
            pl.BlockSpec((HEAD_DIM, width), lambda h: (h, 0)),
            head(0), head(heads), head(0), head(0), head(0),
            pl.BlockSpec((1, length, 1), lambda h: (m * heads + h, 0, 0)),
            column, column, gain, gain, angle, angle, column, keys,
            pl.BlockSpec((length, length), lambda h: (0, 0)),
        ],
        out_specs=[out, out, out, gain, gain, pl.BlockSpec((2, length), lambda h: (0, 0))],
        out_shape=[
            jax.ShapeDtypeStruct((length, cols), f32),
            jax.ShapeDtypeStruct((length, cols), f32),
            jax.ShapeDtypeStruct((length, cols), bf16),
            jax.ShapeDtypeStruct((1, cols), f32),
            jax.ShapeDtypeStruct((1, cols), f32),
            jax.ShapeDtypeStruct((2, length), f32),
        ],
    )(dh, w_o, linear, linear, q_r, k_r, v_r, lse, q_inv, k_inv, gain_q, gain_k, cos, sin,
      ids.reshape(micro * length, 1), ids[:, None, :], order)


def project_back_body(wq_ref, wk_ref, dv_ref, q_ref, k_ref, qi_ref, ki_ref, sum_ref, order_ref, out_ref):
    cols = wq_ref.shape[1]
    q_inv = qi_ref[...]
    k_inv = ki_ref[...]
    total = sum_ref[0] + sum_ref[1] + sum_ref[2] + sum_ref[3]
    total = exact(order_ref[...], total, 1) * (1.0 / (4 * cols))
    out_ref[:, :cols] = (q_inv * (wq_ref[...] - q_ref[...] * (q_inv * total[:, :1]))).astype(bf16)
    out_ref[:, cols : 2 * cols] = (k_inv * (wk_ref[...] - k_ref[...] * (k_inv * total[:, 1:]))).astype(bf16)
    out_ref[:, 2 * cols :] = dv_ref[...]


def project_back(m, w_q, w_k, d_v, linear, q_inv, k_inv, sums, order):
    length, cols = w_q.shape
    rows = length // 2
    full = pl.BlockSpec((rows, cols), lambda i: (i, 0))
    column = pl.BlockSpec((rows, 1), lambda i: (2 * m + i, 0))
    return pl.pallas_call(
        project_back_body,
        grid=(2,),
        in_specs=[full, full, full]
        + [pl.BlockSpec((rows, cols), lambda i, b=b: (2 * m + i, b)) for b in range(2)]
        + [column, column, pl.BlockSpec(sums.shape, lambda i: (0, 0, 0)), pl.BlockSpec((rows, length), lambda i: (i, 0))],
        out_specs=pl.BlockSpec((rows, 3 * cols), lambda i: (i, 0)),
        out_shape=jax.ShapeDtypeStruct((length, 3 * cols), bf16),
    )(w_q, w_k, d_v, linear, linear, q_inv, k_inv, sums, order)


def expert_body(slot_ref, bo_ref, bn_ref, do_ref, dn_ref, wg_ref, wu_ref, wd_ref, router_ref, mine_ref,
                x_ref, act_ref, dy_ref, dgl_ref, dul_ref, oo_ref, on_ref, go_ref, gn_ref, part_ref):
    group = slot_ref.shape[0]
    pack = x_ref.shape[1]
    tok, width = bo_ref.shape[-2:]
    router = router_ref[...]
    mine = mine_ref[...]
    picks, gates, xs, dos, pis, bs = [], [], [], [], [], []
    for g in range(group):
        both = lambda own, near: jnp.concatenate([own[g].reshape(tok, width), near[g].reshape(tok, width)], axis=0)
        b = both(bo_ref, bn_ref)
        logits = nt(router, b)
        weight = jnp.exp(logits - jnp.max(logits, axis=0, keepdims=True))
        pi = weight / jnp.sum(weight, axis=0, keepdims=True)
        slots = lax.broadcasted_iota(jnp.int32, (pack, 2 * tok), 0)
        pick = jnp.where(slots == slot_ref[g], 1.0, 0.0)
        gate = jnp.sum(pi * mine, axis=0, keepdims=True)
        gates.append((gate, jnp.sum(pick * gate, axis=1, keepdims=True)))
        low = pick.astype(bf16)
        picks.append((pick, low))
        xs.append(nn(low, b).astype(bf16))
        dos.append(nn(low, both(do_ref, dn_ref)))
        pis.append(pi)
        bs.append(b)
    x = jnp.concatenate(xs, axis=0)
    gate_p = jnp.concatenate([g[1] for g in gates], axis=0)
    gl = nn(x, wg_ref[...])
    ul = nn(x, wu_ref[...])
    sg = 1.0 / (1.0 + jnp.exp(-gl))
    silu = gl * sg
    act = (silu * ul).astype(bf16)
    do_p = jnp.concatenate(dos, axis=0)
    dy = (gate_p * do_p).astype(bf16)
    y = nn(act, wd_ref[...]).astype(bf16).astype(f32)
    dgate_p = jnp.sum(y * do_p, axis=1, keepdims=True)
    weighted = (gate_p * y).astype(bf16)
    dact = nt(dy, wd_ref[...])
    dgl = (dact * ul * sg * (1.0 + gl * (1.0 - sg))).astype(bf16)
    dul = (dact * silu).astype(bf16)
    drow = (nt(dgl, wg_ref[...]) + nt(dul, wu_ref[...])).astype(bf16)
    total = None
    for g in range(group):
        rows = slice(g * pack, (g + 1) * pack)
        pick, low = picks[g]
        x_ref[g] = x[rows]
        act_ref[g] = act[rows]
        dy_ref[g] = dy[rows]
        dgl_ref[g] = dgl[rows]
        dul_ref[g] = dul[rows]
        out = tn(low, weighted[rows]).astype(bf16)
        oo_ref[g] = out[:tok]
        on_ref[g] = out[tok:]
        dgate = jnp.sum(pick * dgate_p[rows], axis=0, keepdims=True)
        dz = (dgate * gates[g][0] * (mine - pis[g])).astype(bf16)
        grad = (tn(low, drow[rows]) + tn(dz, router)).astype(bf16)
        go_ref[g] = grad[:tok]
        gn_ref[g] = grad[tok:]
        part = nn(dz, bs[g])
        total = part if total is None else total + part

    @pl.when(pl.program_id(0) == 0)
    def _():
        part_ref[...] = total

    @pl.when(pl.program_id(0) > 0)
    def _():
        part_ref[...] = part_ref[...] + total


def expert_step(slot, b_own, b_near, do_own, do_near, gate_w, up_w, down_w, router_t, mine, pack):
    group = 2
    owners = slot.shape[0]
    width, hidden = gate_w.shape
    tok = slot.shape[2] // 2
    experts = router_t.shape[0]

    def rows_spec(value):
        if isinstance(value, tuple):
            at = value[1]
            return pl.BlockSpec((group, 1, tok, width), lambda i: (i, at, 0, 0))
        return pl.BlockSpec((group, tok, width), lambda i: (i, 0, 0))

    def fixed(shape):
        return pl.BlockSpec(shape, lambda i: (0, 0), pipeline_mode=pl.Buffered(1))

    def packed(cols):
        return pl.BlockSpec((group, pack, cols), lambda i: (i, 0, 0))

    token = pl.BlockSpec((group, tok, width), lambda i: (i, 0, 0))
    values = (b_own, b_near, do_own, do_near)
    widths = (width, hidden, width, hidden, hidden)
    return pl.pallas_call(
        expert_body,
        grid=(owners // group,),
        in_specs=[pl.BlockSpec((group, 1, 2 * tok), lambda i: (i, 0, 0))]
        + [rows_spec(v) for v in values]
        + [fixed(gate_w.shape), fixed(up_w.shape), fixed(down_w.shape), fixed(router_t.shape), fixed(mine.shape)],
        out_specs=[packed(c) for c in widths] + [token] * 4 + [pl.BlockSpec((experts, width), lambda i: (0, 0))],
        out_shape=[jax.ShapeDtypeStruct((owners, pack, c), bf16) for c in widths]
        + [jax.ShapeDtypeStruct((owners, tok, width), bf16)] * 4
        + [jax.ShapeDtypeStruct((experts, width), f32)],
        compiler_params=pltpu.CompilerParams(vmem_limit_bytes=60 * 1024 * 1024),
    )(slot, *[v[0] if isinstance(v, tuple) else v for v in values], gate_w, up_w, down_w, router_t, mine)


def half_expert(weight, core):
    other = lax.dynamic_index_in_dim(weight, 1 - core, 0, keepdims=True)
    return lax.dynamic_update_slice(weight, swap_core(other), (1 - core, 0, 0))


def whole_expert(half, side):
    far = swap_side(half)
    whole = jnp.concatenate([half, half], axis=0)
    whole = lax.dynamic_update_slice(whole, far, (2 * (1 - side), 0, 0))
    return whole.reshape(4 * half.shape[1], half.shape[2])


def send_side(grad, side):
    grad = grad.reshape(4, grad.shape[0] // 4, grad.shape[1])
    return swap_side(lax.dynamic_slice_in_dim(grad, 2 * (1 - side), 2, 0).astype(bf16))


def share_expert_grad(grad, far, core, side):
    grad = grad.reshape(4, grad.shape[0] // 4, grad.shape[1])
    mine = lax.dynamic_slice_in_dim(grad, 2 * side, 2, 0) + far.astype(f32)
    near = swap_core(lax.dynamic_index_in_dim(mine, 1 - core, 0, keepdims=True).astype(bf16))
    return lax.dynamic_update_slice(mine, near.astype(f32), (1 - core, 0, 0))


def local(
    tokens,
    cotangent,
    block_ids,
    routes,
    w_query,
    w_key,
    w_value,
    w_out,
    router,
    attention_gain,
    query_gain,
    key_gain,
    mixture_gain,
    w_gate,
    w_up,
    w_down,
):
    micro, tok, width = tokens.shape
    owners = lax.axis_size("expert")
    experts = router.shape[1]
    capacity = (tok * routes.shape[2] * 9 + 8 * experts - 1) // (8 * experts)
    pack = (2 * capacity + 15) // 16 * 16
    rows = w_query.shape[0]
    cols = width // 4
    heads = HEADS // 4
    length = 4 * tok
    s_index = lax.axis_index("shard")
    e_index = lax.axis_index("expert")
    core = s_index % 2
    side = s_index // 2
    my_expert = 2 * e_index + core

    top = routes.shape[2]
    route_cols = micro * tok * top // rows
    used = 4 + experts + route_cols
    aux_cols = (used + 127) // 128 * 128
    aux = jnp.concatenate(
        [
            jnp.stack([attention_gain, query_gain, key_gain, mixture_gain], axis=1),
            router,
            routes.astype(bf16).transpose(0, 2, 1).reshape(rows, route_cols),
            jnp.zeros((rows, aux_cols - used), bf16),
        ],
        axis=1,
    )
    blocks = [w.reshape(rows, 4, cols) for w in (w_query, w_key, w_value)]
    blocks.append(jnp.broadcast_to(aux[:, None, :], (rows, 4, aux_cols)))
    payload = jnp.concatenate(blocks, axis=2).transpose(1, 0, 2)
    payload = lax.all_to_all(payload, "shard", split_axis=0, concat_axis=0, tiled=True)
    do_got = lax.all_gather(cotangent[0], "expert", axis=0, axis_index_groups=low_groups())
    payload, do_got = tie(payload, do_got)
    front = lax.all_gather(payload.reshape(4 * rows, 3 * cols + aux_cols), "expert", axis=0, tiled=True)

    gate_w = whole_expert(half_expert(w_gate, core), side)
    down_w = whole_expert(half_expert(w_down, core), side)
    chunks = gather_shard(tokens)
    devices = 4 * owners
    moves = [(b, (b % owners) * 4 + b // owners) for b in range(devices)]
    w_o_block = lax.ppermute(w_out, BOTH, moves)
    x_all = jnp.concatenate(chunks, axis=1).reshape(micro * length, width)
    x_scale = inverse_rms(x_all.astype(f32))
    chunk_ids = [jnp.bitwise_xor(s_index, j) for j in range(4)]
    positions = jnp.concatenate([c * tok + jnp.arange(tok, dtype=jnp.int32) for c in chunk_ids])
    order = (positions[:, None] == jnp.arange(length)[None, :]).astype(f32)
    rate = ROPE_BASE ** (-2.0 * jnp.arange(HEAD_DIM // 2, dtype=f32) / HEAD_DIM)
    angles = positions.astype(f32)[:, None] * rate[None, :]
    cosine = jnp.cos(angles)
    sine = jnp.sin(angles)
    cosine = jnp.concatenate([cosine, cosine], axis=1)
    sine = jnp.concatenate([-sine, sine], axis=1)
    up_w = whole_expert(half_expert(w_up, core), side)
    front, gate_w, up_w, w_o_block, x_all, x_scale, cosine, sine = tie(
        front, gate_w, up_w, w_o_block, x_all, x_scale, cosine, sine
    )
    do_got, more_own, _ = tie(do_got, cotangent[1], front)
    do_other = swap_low(do_got)
    w_o = lax.all_gather(w_o_block, "expert", axis=0, tiled=True)
    w_qkv = front[:, : 3 * cols]
    aux_rows = front[:, 3 * cols :].T.astype(f32)
    gain_attention = aux_rows[0]
    gain_query = lax.dynamic_slice_in_dim(aux_rows[1], s_index * cols, cols)
    gain_key = lax.dynamic_slice_in_dim(aux_rows[2], s_index * cols, cols)
    gain_mixture = aux_rows[3]


    all_routes = front[:, 3 * cols + 4 + experts : 3 * cols + used].astype(jnp.int32)
    all_routes = all_routes.reshape(owners, 4, micro, top, tok)
    mine = all_routes == my_expert
    mine = jnp.any(mine, axis=3)
    pair = [lax.dynamic_index_in_dim(mine, s_index ^ j, 1, keepdims=False) for j in range(2)]
    mask = jnp.concatenate(pair, axis=2).transpose(1, 0, 2)
    places = jnp.arange(2 * tok)
    earlier = (places[:, None] < places[None, :]).astype(bf16)
    slot = jnp.einsum("met,tu->meu", mask.astype(bf16), earlier, preferred_element_type=f32)
    slot = jnp.where(mask, slot.astype(jnp.int32), -1)
    slot = slot[:, :, None, :]

    a_all = (x_all.astype(f32) * x_scale * gain_attention).astype(bf16)
    linear = nn(a_all, w_qkv)
    q_lin = linear[:, :cols]
    k_lin = linear[:, cols : 2 * cols]
    sums = jnp.stack([jnp.sum(q_lin * q_lin, axis=1), jnp.sum(k_lin * k_lin, axis=1)])
    sums = sum_rows(sums, core, side, tok)
    inv = lax.rsqrt(sums / width + EPSILON)
    q_inv = inv[0][:, None]
    k_inv = inv[1][:, None]
    ids = block_ids[:, 0, :]
    ids = jnp.concatenate(
        [lax.dynamic_slice_in_dim(ids, c * tok, tok, axis=1) for c in chunk_ids], axis=1
    )
    gain_query = gain_query[None, :]
    gain_key = gain_key[None, :]
    q_r, k_r, v_r, o_all, lse = attend(
        linear, q_inv, k_inv, gain_query, gain_key, cosine, sine, ids, heads
    )
    branch = nn(o_all, w_o).reshape(micro, 4, tok, width)
    branch = scatter_shard([branch[:, j] for j in range(4)])
    hidden = tokens.astype(f32) + branch
    h_scale = inverse_rms(hidden)
    h_n = hidden * h_scale
    b_own = (h_n * gain_mixture).astype(bf16)

    def gather_expert(own):
        return lax.all_gather(own, "expert", axis=0, tiled=True)

    my_expert = 2 * e_index + core
    low = e_index % 2
    do_first = jnp.stack(
        [jnp.where(low == 0, do_got, do_other), jnp.where(low == 0, do_other, do_got)], axis=1
    ).reshape(owners, tok, width)
    more = lax.all_gather(more_own, "expert", axis=0, axis_index_groups=low_groups())
    b_own, more = tie(b_own, more)
    b_first = gather_expert(b_own[0][None])
    second = gather_expert(b_own[1][None])
    b_first, down_w = tie(b_first, down_w)
    out_parts = []
    db_list = []
    kept = []
    router_t = front[:, 3 * cols + 4 : 3 * cols + 4 + experts].T
    is_mine = (jnp.arange(experts) == my_expert).astype(f32)[:, None]
    router_part = jnp.zeros((experts, width), f32)
    for m in range(micro):
        if m == 0:
            values = (b_first, swap_core(b_first), do_first, swap_core(do_first))
        else:
            second, more, _ = tie(second, more, db_half)
            more_other = swap_low(more)
            do_second = jnp.stack(
                [jnp.where(low == 0, more, more_other), jnp.where(low == 0, more_other, more)], axis=1
            ).reshape(owners, tok, width)
            values = (second, swap_core(second), do_second, swap_core(do_second))
        *saved, out_mine, out_near, db_mine, db_near, part = expert_step(
            slot[m], *values, gate_w, up_w, down_w, router_t, is_mine, pack
        )
        router_part = router_part + part
        db_half = (db_mine.astype(f32) + swap_core(db_near).astype(f32)).astype(bf16)
        db_list.append(lax.psum_scatter(db_half, "expert", scatter_dimension=0, tiled=True)[0])
        out_parts.append((out_mine, out_near))
        kept.append([v.reshape(owners * pack, v.shape[2]) for v in saved])
    x_k, act_k, dy_k, dgl_k, dul_k = [jnp.concatenate(group, axis=0) for group in zip(*kept)]
    outs = [v for pair in out_parts for v in pair]
    _, db_list[0], x_k, act_k, *outs = tie(db_half, db_list[0], x_k, act_k, *outs)
    out_parts = [
        (outs[2 * m].astype(f32) + swap_core(outs[2 * m + 1]).astype(f32)).astype(bf16) for m in range(micro)
    ]
    full_gate = tn(x_k, dgl_k)
    full_up = tn(x_k, dul_k)
    full_down = tn(act_k, dy_k)
    mixture_part = jnp.zeros((width,), f32)
    query_part = jnp.zeros((cols,), f32)
    key_part = jnp.zeros((cols,), f32)
    x_own = tokens.astype(f32)
    own_scale = inverse_rms(x_own)
    dh_rows = []
    dqkv_rows = []
    d_hiddens = []
    input_grads = []
    for m in range(micro):
        db = db_list[m].astype(f32)
        mixture_part = mixture_part + jnp.sum(db * h_n[m], axis=0)
        w_g = db * gain_mixture
        d_hidden = cotangent[m].astype(f32) + h_scale[m] * (
            w_g - h_n[m] * jnp.mean(w_g * h_n[m], axis=-1, keepdims=True)
        )
        dh_m = jnp.concatenate(gather_shard(d_hidden.astype(bf16)), axis=0)
        if m == 0:
            out_part = jnp.stack(out_parts, axis=1)
            dh_m, full_gate, full_up, full_down, out_part = tie(dh_m, full_gate, full_up, full_down, out_part)
        dh_rows.append(dh_m)
        w_q, w_k, d_v, part_q, part_k, sums = attend_back(
            m, dh_m, w_o, linear, q_r, k_r, v_r, lse, q_inv, k_inv, gain_query, gain_key, cosine, sine, ids, order, heads
        )
        query_part = query_part + part_q[0]
        key_part = key_part + part_k[0]
        sums = lax.all_gather(sums, "shard", axis=0)
        d_qkv = project_back(m, w_q, w_k, d_v, linear, q_inv, k_inv, sums, order)
        if m + 1 < micro:
            db_list[m + 1], d_qkv, out_part = tie(db_list[m + 1], d_qkv, out_part)
            out_own = lax.psum_scatter(out_part, "expert", scatter_dimension=0, tiled=True)[0]
        dqkv_rows.append(d_qkv)
        d_hiddens.append(d_hidden)
    dh_all = jnp.concatenate(dh_rows, axis=0)
    grad_wo = jnp.stack(
        [tn(o_all, dh_all[:, i * cols : (i + 1) * cols]).astype(bf16).reshape(owners, rows, cols) for i in range(4)],
        axis=1,
    ).reshape(width, cols)

    blank = jnp.zeros((width,), f32)
    gains = jnp.stack(
        [
            blank,
            lax.dynamic_update_slice(blank, query_part, (s_index * cols,)),
            lax.dynamic_update_slice(blank, key_part, (s_index * cols,)),
            mixture_part,
        ],
        axis=1,
    )
    (aux_grad,) = tie(
        jnp.concatenate([gains, router_part.T, jnp.zeros((width, aux_cols - 4 - experts), f32)], axis=1).astype(bf16)
    )
    grad_payload = jnp.concatenate([tn(a_all, jnp.concatenate(dqkv_rows, axis=0)).astype(bf16), grad_wo, aux_grad], axis=1)
    grad_payload, out_own, *dqkv_rows = tie(grad_payload, out_own, *dqkv_rows)
    grad_own = lax.psum_scatter(grad_payload, "expert", scatter_dimension=0, tiled=True)
    output = (hidden + out_own.astype(f32)).astype(bf16)
    for m in range(micro):
        da_part = nt(dqkv_rows[m], w_qkv)
        da_part = da_part.reshape(4, tok, width)
        da = scatter_shard([da_part[j] for j in range(4)])
        da, full_gate, full_up, full_down = tie(da, full_gate, full_up, full_down)
        x_n = x_own[m] * own_scale[m]
        a_g = da * gain_attention
        grad = d_hiddens[m] + own_scale[m] * (a_g - x_n * jnp.mean(a_g * x_n, axis=-1, keepdims=True))
        input_grads.append(grad.astype(bf16))
    input_grad = jnp.stack(input_grads)
    sent_gate = send_side(full_gate, side)
    sent_up = send_side(full_up, side)
    sent_down = send_side(full_down, side)
    grad_gate = share_expert_grad(full_gate, sent_gate, core, side)
    grad_up = share_expert_grad(full_up, sent_up, core, side)
    grad_down = share_expert_grad(full_down, sent_down, core, side)
    grad_own = grad_own.reshape(4, rows, 4 * cols + aux_cols)
    grad_wo = grad_own[:, :, 3 * cols : 4 * cols].transpose(1, 0, 2).reshape(rows, width)
    grad_wo = lax.ppermute(grad_wo, BOTH, [(d, b) for b, d in moves]).astype(f32)
    grad_own = jnp.concatenate([grad_own[:, :, : 3 * cols], grad_own[:, :, 4 * cols :]], axis=2)
    grad_own = lax.all_to_all(grad_own, "shard", split_axis=0, concat_axis=0, tiled=True).astype(f32)
    grad_q, grad_k, grad_v = [
        grad_own[:, :, i * cols : (i + 1) * cols].transpose(1, 0, 2).reshape(rows, width)
        for i in range(3)
    ]
    aux_sum = jnp.sum(grad_own[:, :, 3 * cols :], axis=0)
    grad_gain = sum(
        jnp.sum(w.astype(f32) * g, axis=1) for w, g in ((w_query, grad_q), (w_key, grad_k), (w_value, grad_v))
    )
    grad_gain = grad_gain / attention_gain.astype(f32)
    return (
        output,
        input_grad,
        grad_q,
        grad_k,
        grad_v,
        grad_wo,
        aux_sum[:, 4 : 4 + experts],
        grad_gain,
        aux_sum[:, 1],
        aux_sum[:, 2],
        aux_sum[:, 3],
        grad_gate,
        grad_up,
        grad_down,
    )


def solution(mesh):
    tokens_spec = P(None, BOTH, None)
    rows_spec = P(BOTH, None)
    gain_spec = P(BOTH)
    expert_spec = P("expert", "shard", None)
    return jax.shard_map(
        local,
        mesh=mesh,
        in_specs=(tokens_spec, tokens_spec, P(None, "expert", None), tokens_spec)
        + (rows_spec,) * 5
        + (gain_spec,) * 4
        + (expert_spec,) * 3,
        out_specs=(tokens_spec, tokens_spec)
        + (rows_spec,) * 5
        + (gain_spec,) * 4
        + (expert_spec,) * 3,
        check_vma=False,
    )
```

```python
import jax
import jax.numpy as jnp
from jax import lax
from jax.experimental import pallas as pl
from jax.experimental.pallas import tpu as pltpu
from jax.sharding import PartitionSpec as P

HEADS = 16
HEAD_DIM = 128
EPSILON = 1e-05
ROPE_BASE = 10000.0
MASKED = -1e30
BOTH = ("expert", "shard")

f32 = jnp.float32
bf16 = jnp.bfloat16


def dot(left, right, dims):
    return lax.dot_general(left, right, (dims, ((), ())), preferred_element_type=f32)


def nn(left, right):
    return dot(left, right, ((1,), (0,)))


def nt(left, right):
    return dot(left, right, ((1,), (1,)))


def tn(left, right):
    return dot(left, right, ((0,), (0,)))


def swap_core(values):
    return lax.ppermute(values, "shard", [(s, s ^ 1) for s in range(4)])


def swap_side(values):
    return lax.ppermute(values, "shard", [(s, s ^ 2) for s in range(4)])


def gather_shard(values):
    near = swap_core(values)
    far = swap_side(values)
    return [values, near, far, swap_core(far)]


def scatter_shard(parts):
    near = swap_core(jnp.stack([parts[1], parts[3]]).astype(bf16)).astype(f32)
    far = swap_side((parts[2] + near[1]).astype(bf16)).astype(f32)
    return parts[0] + near[0] + far


def tie(*values):
    return lax.optimization_barrier(values)


def low_groups():
    count = lax.axis_size("expert")
    return [[2 * h + low for h in range(count // 2)] for low in range(2)]


def swap_low(values):
    count = lax.axis_size("expert")
    return lax.ppermute(values, "expert", [(e, e ^ 1) for e in range(count)])


def sum_rows(values, core, side, tok):
    def reorder(v):
        v = v.reshape(2, -1, 2, 2, tok)
        v = jnp.where(core == 1, jnp.concatenate([v[:, :, :, 1:], v[:, :, :, :1]], axis=3), v)
        v = jnp.where(side == 1, jnp.concatenate([v[:, :, 1:], v[:, :, :1]], axis=2), v)
        return v.reshape(values.shape)

    return reorder(jnp.sum(lax.all_gather(reorder(values), "shard", axis=0), axis=0))


def inverse_rms(values):
    return lax.rsqrt(jnp.mean(values * values, axis=-1, keepdims=True) + EPSILON)


def attend_body(q_ref, k_ref, v_ref, qi_ref, ki_ref, gq_ref, gk_ref, cos_ref, sin_ref, idq_ref, idk_ref,
                qr_ref, kr_ref, vr_ref, o_ref, lse_ref):
    cos = cos_ref[...]
    sin = sin_ref[...]
    half = HEAD_DIM // 2

    def rope(values):
        return (values * cos + pltpu.roll(values, half, 1) * sin).astype(bf16)

    q_r = rope(q_ref[...] * qi_ref[...] * gq_ref[...])
    k_r = rope(k_ref[...] * ki_ref[...] * gk_ref[...])
    v_r = v_ref[...].astype(bf16)
    qr_ref[...] = q_r
    kr_ref[...] = k_r
    vr_ref[...] = v_r
    scores = jnp.where(idk_ref[0] <= idq_ref[...], nt(q_r, k_r) * HEAD_DIM ** (-0.5), MASKED)
    peak = jnp.max(scores, axis=-1, keepdims=True)
    weight = jnp.exp(scores - peak)
    total = jnp.sum(weight, axis=-1, keepdims=True)
    o_ref[...] = nn((weight / total).astype(bf16), v_r).astype(bf16)
    lse_ref[0] = peak + jnp.log(total)


def attend(linear, q_inv, k_inv, gain_q, gain_k, cos, sin, ids, heads):
    micro, length = ids.shape
    cols = heads * HEAD_DIM
    total = micro * length
    head = lambda base: pl.BlockSpec((length, HEAD_DIM), lambda m, h: (m, base + h))
    column = pl.BlockSpec((length, 1), lambda m, h: (m, 0))
    gain = pl.BlockSpec((1, HEAD_DIM), lambda m, h: (0, h))
    angle = pl.BlockSpec((length, HEAD_DIM), lambda m, h: (0, 0))
    keys = pl.BlockSpec((1, 1, length), lambda m, h: (m, 0, 0))
    low = jax.ShapeDtypeStruct((total, cols), bf16)
    return pl.pallas_call(
        attend_body,
        grid=(micro, heads),
        in_specs=[head(0), head(heads), head(2 * heads), column, column, gain, gain, angle, angle, column, keys],
        out_specs=[head(0)] * 4 + [pl.BlockSpec((1, length, 1), lambda m, h: (m * heads + h, 0, 0))],
        out_shape=[low] * 4 + [jax.ShapeDtypeStruct((micro * heads, length, 1), f32)],
    )(linear, linear, linear, q_inv, k_inv, gain_q, gain_k, cos, sin, ids.reshape(total, 1), ids[:, None, :])


def exact(left, right, at):
    dims = (((1,), (at,)), ((), ()))
    return lax.dot_general(left, right, dims, precision=lax.Precision.HIGHEST, preferred_element_type=f32)


def attend_back_body(dh_ref, wo_ref, q_ref, k_ref, qr_ref, kr_ref, vr_ref, lse_ref, qi_ref, ki_ref, gq_ref, gk_ref,
                     cos_ref, sin_ref, idq_ref, idk_ref, order_ref, wq_ref, wk_ref, dv_ref, pq_ref, pk_ref, sum_ref):
    cos = cos_ref[...]
    sin = sin_ref[...]
    half = HEAD_DIM // 2
    scale = HEAD_DIM ** (-0.5)
    q_r = qr_ref[...]
    k_r = kr_ref[...]
    d_o = nt(dh_ref[...], wo_ref[...]).astype(bf16)
    scores = jnp.where(idk_ref[0] <= idq_ref[...], nt(q_r, k_r) * scale, MASKED)
    prob = jnp.exp(scores - lse_ref[0])
    d_prob = nt(d_o, vr_ref[...])
    delta = jnp.sum(prob * d_prob, axis=-1, keepdims=True)
    d_s = (prob * (d_prob - delta)).astype(bf16)
    dv_ref[...] = tn(prob.astype(bf16), d_o).astype(bf16)
    ones = jnp.ones((8, HEAD_DIM), f32)

    def finish(grad, linear, inverse, gain, out_ref, part_ref, at):
        grad = grad * scale
        grad = grad * cos - pltpu.roll(grad, half, 1) * sin
        normed = linear * inverse
        part_ref[...] = jnp.sum(grad * normed, axis=0, keepdims=True)
        grad = grad * gain
        out_ref[...] = grad
        rows = exact(ones, grad * normed, 1)

        rows = exact(rows, order_ref[...], 0)[:1]

        @pl.when(pl.program_id(0) == 0)
        def _():
            sum_ref[at : at + 1] = rows

        @pl.when(pl.program_id(0) > 0)
        def _():
            sum_ref[at : at + 1] = sum_ref[at : at + 1] + rows

    finish(nn(d_s, k_r), q_ref[...], qi_ref[...], gq_ref[...], wq_ref, pq_ref, 0)
    finish(tn(d_s, q_r), k_ref[...], ki_ref[...], gk_ref[...], wk_ref, pk_ref, 1)


def attend_back(m, dh, w_o, linear, q_r, k_r, v_r, lse, q_inv, k_inv, gain_q, gain_k, cos, sin, ids, order, heads):
    micro, length = ids.shape
    cols = heads * HEAD_DIM
    width = dh.shape[1]
    head = lambda base: pl.BlockSpec((length, HEAD_DIM), lambda h: (m, base + h))
    column = pl.BlockSpec((length, 1), lambda h: (m, 0))
    gain = pl.BlockSpec((1, HEAD_DIM), lambda h: (0, h))
    angle = pl.BlockSpec((length, HEAD_DIM), lambda h: (0, 0))
    keys = pl.BlockSpec((1, 1, length), lambda h: (m, 0, 0))
    out = pl.BlockSpec((length, HEAD_DIM), lambda h: (0, h))
    return pl.pallas_call(
        attend_back_body,
        grid=(heads,),
        in_specs=[
            pl.BlockSpec((length, width), lambda h: (0, 0)),
            pl.BlockSpec((HEAD_DIM, width), lambda h: (h, 0)),
            head(0), head(heads), head(0), head(0), head(0),
            pl.BlockSpec((1, length, 1), lambda h: (m * heads + h, 0, 0)),
            column, column, gain, gain, angle, angle, column, keys,
            pl.BlockSpec((length, length), lambda h: (0, 0)),
        ],
        out_specs=[out, out, out, gain, gain, pl.BlockSpec((2, length), lambda h: (0, 0))],
        out_shape=[
            jax.ShapeDtypeStruct((length, cols), f32),
            jax.ShapeDtypeStruct((length, cols), f32),
            jax.ShapeDtypeStruct((length, cols), bf16),
            jax.ShapeDtypeStruct((1, cols), f32),
            jax.ShapeDtypeStruct((1, cols), f32),
            jax.ShapeDtypeStruct((2, length), f32),
        ],
    )(dh, w_o, linear, linear, q_r, k_r, v_r, lse, q_inv, k_inv, gain_q, gain_k, cos, sin,
      ids.reshape(micro * length, 1), ids[:, None, :], order)


def project_back_body(wq_ref, wk_ref, dv_ref, q_ref, k_ref, qi_ref, ki_ref, sum_ref, order_ref, out_ref):
    cols = wq_ref.shape[1]
    q_inv = qi_ref[...]
    k_inv = ki_ref[...]
    total = sum_ref[0] + sum_ref[1] + sum_ref[2] + sum_ref[3]
    total = exact(order_ref[...], total, 1) * (1.0 / (4 * cols))
    out_ref[:, :cols] = (q_inv * (wq_ref[...] - q_ref[...] * (q_inv * total[:, :1]))).astype(bf16)
    out_ref[:, cols : 2 * cols] = (k_inv * (wk_ref[...] - k_ref[...] * (k_inv * total[:, 1:]))).astype(bf16)
    out_ref[:, 2 * cols :] = dv_ref[...]


def project_back(m, w_q, w_k, d_v, linear, q_inv, k_inv, sums, order):
    length, cols = w_q.shape
    rows = length // 2
    full = pl.BlockSpec((rows, cols), lambda i: (i, 0))
    column = pl.BlockSpec((rows, 1), lambda i: (2 * m + i, 0))
    return pl.pallas_call(
        project_back_body,
        grid=(2,),
        in_specs=[full, full, full]
        + [pl.BlockSpec((rows, cols), lambda i, b=b: (2 * m + i, b)) for b in range(2)]
        + [column, column, pl.BlockSpec(sums.shape, lambda i: (0, 0, 0)), pl.BlockSpec((rows, length), lambda i: (i, 0))],
        out_specs=pl.BlockSpec((rows, 3 * cols), lambda i: (i, 0)),
        out_shape=jax.ShapeDtypeStruct((length, 3 * cols), bf16),
    )(w_q, w_k, d_v, linear, linear, q_inv, k_inv, sums, order)


def expert_body(slot_ref, bo_ref, bn_ref, do_ref, dn_ref, wg_ref, wu_ref, wd_ref, router_ref, mine_ref,
                x_ref, act_ref, dy_ref, dgl_ref, dul_ref, oo_ref, on_ref, go_ref, gn_ref, part_ref):
    group = slot_ref.shape[0]
    pack = x_ref.shape[1]
    tok, width = bo_ref.shape[-2:]
    router = router_ref[...]
    mine = mine_ref[...]
    picks, gates, xs, dos, pis, bs = [], [], [], [], [], []
    for g in range(group):
        both = lambda own, near: jnp.concatenate([own[g].reshape(tok, width), near[g].reshape(tok, width)], axis=0)
        b = both(bo_ref, bn_ref)
        logits = nt(router, b)
        weight = jnp.exp(logits - jnp.max(logits, axis=0, keepdims=True))
        pi = weight / jnp.sum(weight, axis=0, keepdims=True)
        slots = lax.broadcasted_iota(jnp.int32, (pack, 2 * tok), 0)
        pick = jnp.where(slots == slot_ref[g], 1.0, 0.0)
        gate = jnp.sum(pi * mine, axis=0, keepdims=True)
        gates.append((gate, jnp.sum(pick * gate, axis=1, keepdims=True)))
        low = pick.astype(bf16)
        picks.append((pick, low))
        xs.append(nn(low, b).astype(bf16))
        dos.append(nn(low, both(do_ref, dn_ref)))
        pis.append(pi)
        bs.append(b)
    x = jnp.concatenate(xs, axis=0)
    gate_p = jnp.concatenate([g[1] for g in gates], axis=0)
    gl = nn(x, wg_ref[...])
    ul = nn(x, wu_ref[...])
    sg = 1.0 / (1.0 + jnp.exp(-gl))
    silu = gl * sg
    act = (silu * ul).astype(bf16)
    do_p = jnp.concatenate(dos, axis=0)
    dy = (gate_p * do_p).astype(bf16)
    y = nn(act, wd_ref[...]).astype(bf16).astype(f32)
    dgate_p = jnp.sum(y * do_p, axis=1, keepdims=True)
    weighted = (gate_p * y).astype(bf16)
    dact = nt(dy, wd_ref[...])
    dgl = (dact * ul * sg * (1.0 + gl * (1.0 - sg))).astype(bf16)
    dul = (dact * silu).astype(bf16)
    drow = (nt(dgl, wg_ref[...]) + nt(dul, wu_ref[...])).astype(bf16)
    total = None
    for g in range(group):
        rows = slice(g * pack, (g + 1) * pack)
        pick, low = picks[g]
        x_ref[g] = x[rows]
        act_ref[g] = act[rows]
        dy_ref[g] = dy[rows]
        dgl_ref[g] = dgl[rows]
        dul_ref[g] = dul[rows]
        out = tn(low, weighted[rows]).astype(bf16)
        oo_ref[g] = out[:tok]
        on_ref[g] = out[tok:]
        dgate = jnp.sum(pick * dgate_p[rows], axis=0, keepdims=True)
        dz = (dgate * gates[g][0] * (mine - pis[g])).astype(bf16)
        grad = (tn(low, drow[rows]) + tn(dz, router)).astype(bf16)
        go_ref[g] = grad[:tok]
        gn_ref[g] = grad[tok:]
        part = nn(dz, bs[g])
        total = part if total is None else total + part

    @pl.when(pl.program_id(0) == 0)
    def _():
        part_ref[...] = total

    @pl.when(pl.program_id(0) > 0)
    def _():
        part_ref[...] = part_ref[...] + total


def expert_step(slot, b_own, b_near, do_own, do_near, gate_w, up_w, down_w, router_t, mine, pack):
    group = 2
    owners = slot.shape[0]
    width, hidden = gate_w.shape
    tok = slot.shape[2] // 2
    experts = router_t.shape[0]

    def rows_spec(value):
        if isinstance(value, tuple):
            at = value[1]
            return pl.BlockSpec((group, 1, tok, width), lambda i: (i, at, 0, 0))
        return pl.BlockSpec((group, tok, width), lambda i: (i, 0, 0))

    def fixed(shape):
        return pl.BlockSpec(shape, lambda i: (0, 0), pipeline_mode=pl.Buffered(1))

    def packed(cols):
        return pl.BlockSpec((group, pack, cols), lambda i: (i, 0, 0))

    token = pl.BlockSpec((group, tok, width), lambda i: (i, 0, 0))
    values = (b_own, b_near, do_own, do_near)
    widths = (width, hidden, width, hidden, hidden)
    return pl.pallas_call(
        expert_body,
        grid=(owners // group,),
        in_specs=[pl.BlockSpec((group, 1, 2 * tok), lambda i: (i, 0, 0))]
        + [rows_spec(v) for v in values]
        + [fixed(gate_w.shape), fixed(up_w.shape), fixed(down_w.shape), fixed(router_t.shape), fixed(mine.shape)],
        out_specs=[packed(c) for c in widths] + [token] * 4 + [pl.BlockSpec((experts, width), lambda i: (0, 0))],
        out_shape=[jax.ShapeDtypeStruct((owners, pack, c), bf16) for c in widths]
        + [jax.ShapeDtypeStruct((owners, tok, width), bf16)] * 4
        + [jax.ShapeDtypeStruct((experts, width), f32)],
        compiler_params=pltpu.CompilerParams(vmem_limit_bytes=60 * 1024 * 1024),
    )(slot, *[v[0] if isinstance(v, tuple) else v for v in values], gate_w, up_w, down_w, router_t, mine)


def half_expert(weight, core):
    other = lax.dynamic_index_in_dim(weight, 1 - core, 0, keepdims=True)
    return lax.dynamic_update_slice(weight, swap_core(other), (1 - core, 0, 0))


def whole_expert(half, side):
    far = swap_side(half)
    whole = jnp.concatenate([half, half], axis=0)
    whole = lax.dynamic_update_slice(whole, far, (2 * (1 - side), 0, 0))
    return whole.reshape(4 * half.shape[1], half.shape[2])


def send_side(grad, side):
    grad = grad.reshape(4, grad.shape[0] // 4, grad.shape[1])
    return swap_side(lax.dynamic_slice_in_dim(grad, 2 * (1 - side), 2, 0).astype(bf16))


def share_expert_grad(grad, far, core, side):
    grad = grad.reshape(4, grad.shape[0] // 4, grad.shape[1])
    mine = lax.dynamic_slice_in_dim(grad, 2 * side, 2, 0) + far.astype(f32)
    near = swap_core(lax.dynamic_index_in_dim(mine, 1 - core, 0, keepdims=True).astype(bf16))
    return lax.dynamic_update_slice(mine, near.astype(f32), (1 - core, 0, 0))


def local(
    tokens,
    cotangent,
    block_ids,
    routes,
    w_query,
    w_key,
    w_value,
    w_out,
    router,
    attention_gain,
    query_gain,
    key_gain,
    mixture_gain,
    w_gate,
    w_up,
    w_down,
):
    micro, tok, width = tokens.shape
    owners = lax.axis_size("expert")
    experts = router.shape[1]
    capacity = (tok * routes.shape[2] * 9 + 8 * experts - 1) // (8 * experts)
    pack = (2 * capacity + 15) // 16 * 16
    rows = w_query.shape[0]
    cols = width // 4
    heads = HEADS // 4
    length = 4 * tok
    s_index = lax.axis_index("shard")
    e_index = lax.axis_index("expert")
    core = s_index % 2
    side = s_index // 2
    my_expert = 2 * e_index + core

    top = routes.shape[2]
    route_cols = micro * tok * top // rows
    used = 4 + experts + route_cols
    aux_cols = (used + 127) // 128 * 128
    aux = jnp.concatenate(
        [
            jnp.stack([attention_gain, query_gain, key_gain, mixture_gain], axis=1),
            router,
            routes.astype(bf16).transpose(0, 2, 1).reshape(rows, route_cols),
            jnp.zeros((rows, aux_cols - used), bf16),
        ],
        axis=1,
    )
    blocks = [w.reshape(rows, 4, cols) for w in (w_query, w_key, w_value)]
    blocks.append(jnp.broadcast_to(aux[:, None, :], (rows, 4, aux_cols)))
    payload = jnp.concatenate(blocks, axis=2).transpose(1, 0, 2)
    payload = lax.all_to_all(payload, "shard", split_axis=0, concat_axis=0, tiled=True)
    do_got = lax.all_gather(cotangent[0], "expert", axis=0, axis_index_groups=low_groups())
    payload, do_got = tie(payload, do_got)
    front = lax.all_gather(payload.reshape(4 * rows, 3 * cols + aux_cols), "expert", axis=0, tiled=True)

    gate_w = whole_expert(half_expert(w_gate, core), side)
    down_w = whole_expert(half_expert(w_down, core), side)
    chunks = gather_shard(tokens)
    devices = 4 * owners
    moves = [(b, (b % owners) * 4 + b // owners) for b in range(devices)]
    w_o_block = lax.ppermute(w_out, BOTH, moves)
    x_all = jnp.concatenate(chunks, axis=1).reshape(micro * length, width)
    x_scale = inverse_rms(x_all.astype(f32))
    chunk_ids = [jnp.bitwise_xor(s_index, j) for j in range(4)]
    positions = jnp.concatenate([c * tok + jnp.arange(tok, dtype=jnp.int32) for c in chunk_ids])
    order = (positions[:, None] == jnp.arange(length)[None, :]).astype(f32)
    rate = ROPE_BASE ** (-2.0 * jnp.arange(HEAD_DIM // 2, dtype=f32) / HEAD_DIM)
    angles = positions.astype(f32)[:, None] * rate[None, :]
    cosine = jnp.cos(angles)
    sine = jnp.sin(angles)
    cosine = jnp.concatenate([cosine, cosine], axis=1)
    sine = jnp.concatenate([-sine, sine], axis=1)
    up_w = whole_expert(half_expert(w_up, core), side)
    front, gate_w, up_w, w_o_block, x_all, x_scale, cosine, sine = tie(
        front, gate_w, up_w, w_o_block, x_all, x_scale, cosine, sine
    )
    do_got, _ = tie(do_got, front)
    do_other = swap_low(do_got)
    w_o = lax.all_gather(w_o_block, "expert", axis=0, tiled=True)
    w_qkv = front[:, : 3 * cols]
    aux_rows = front[:, 3 * cols :].T.astype(f32)
    gain_attention = aux_rows[0]
    gain_query = lax.dynamic_slice_in_dim(aux_rows[1], s_index * cols, cols)
    gain_key = lax.dynamic_slice_in_dim(aux_rows[2], s_index * cols, cols)
    gain_mixture = aux_rows[3]


    all_routes = front[:, 3 * cols + 4 + experts : 3 * cols + used].astype(jnp.int32)
    all_routes = all_routes.reshape(owners, 4, micro, top, tok)
    mine = all_routes == my_expert
    mine = jnp.any(mine, axis=3)
    pair = [lax.dynamic_index_in_dim(mine, s_index ^ j, 1, keepdims=False) for j in range(2)]
    mask = jnp.concatenate(pair, axis=2).transpose(1, 0, 2)
    places = jnp.arange(2 * tok)
    earlier = (places[:, None] < places[None, :]).astype(bf16)
    slot = jnp.einsum("met,tu->meu", mask.astype(bf16), earlier, preferred_element_type=f32)
    slot = jnp.where(mask, slot.astype(jnp.int32), -1)
    slot = slot[:, :, None, :]

    a_all = (x_all.astype(f32) * x_scale * gain_attention).astype(bf16)
    linear = nn(a_all, w_qkv)
    q_lin = linear[:, :cols]
    k_lin = linear[:, cols : 2 * cols]
    sums = jnp.stack([jnp.sum(q_lin * q_lin, axis=1), jnp.sum(k_lin * k_lin, axis=1)])
    sums = sum_rows(sums, core, side, tok)
    inv = lax.rsqrt(sums / width + EPSILON)
    q_inv = inv[0][:, None]
    k_inv = inv[1][:, None]
    ids = block_ids[:, 0, :]
    ids = jnp.concatenate(
        [lax.dynamic_slice_in_dim(ids, c * tok, tok, axis=1) for c in chunk_ids], axis=1
    )
    gain_query = gain_query[None, :]
    gain_key = gain_key[None, :]
    q_r, k_r, v_r, o_all, lse = attend(
        linear, q_inv, k_inv, gain_query, gain_key, cosine, sine, ids, heads
    )
    branch = nn(o_all, w_o).reshape(micro, 4, tok, width)
    branch = scatter_shard([branch[:, j] for j in range(4)])
    hidden = tokens.astype(f32) + branch
    h_scale = inverse_rms(hidden)
    h_n = hidden * h_scale
    b_own = (h_n * gain_mixture).astype(bf16)

    def gather_expert(own):
        return lax.all_gather(own, "expert", axis=0, tiled=True)

    my_expert = 2 * e_index + core
    low = e_index % 2
    do_first = jnp.stack(
        [jnp.where(low == 0, do_got, do_other), jnp.where(low == 0, do_other, do_got)], axis=1
    ).reshape(owners, tok, width)
    b_first = gather_expert(b_own[0][None])
    second = gather_expert(jnp.stack([b_own[1], cotangent[1]])[None])
    b_first, down_w = tie(b_first, down_w)
    out_parts = []
    db_list = []
    kept = []
    router_t = front[:, 3 * cols + 4 : 3 * cols + 4 + experts].T
    is_mine = (jnp.arange(experts) == my_expert).astype(f32)[:, None]
    router_part = jnp.zeros((experts, width), f32)
    for m in range(micro):
        if m == 0:
            values = (b_first, swap_core(b_first), do_first, swap_core(do_first))
        else:
            second, _ = tie(second, db_half)
            near = swap_core(second)
            values = ((second, 0), (near, 0), (second, 1), (near, 1))
        *saved, out_mine, out_near, db_mine, db_near, part = expert_step(
            slot[m], *values, gate_w, up_w, down_w, router_t, is_mine, pack
        )
        router_part = router_part + part
        db_half = (db_mine.astype(f32) + swap_core(db_near).astype(f32)).astype(bf16)
        db_list.append(lax.psum_scatter(db_half, "expert", scatter_dimension=0, tiled=True)[0])
        out_parts.append((out_mine, out_near))
        kept.append([v.reshape(owners * pack, v.shape[2]) for v in saved])
    outs = [v for pair in out_parts for v in pair]
    _, db_list[0], kept, *outs = tie(db_half, db_list[0], kept, *outs)
    x_k, act_k, dy_k, dgl_k, dul_k = [jnp.concatenate(group, axis=0) for group in zip(*kept)]
    out_parts = [
        (outs[2 * m].astype(f32) + swap_core(outs[2 * m + 1]).astype(f32)).astype(bf16) for m in range(micro)
    ]
    full_gate = tn(x_k, dgl_k)
    full_up = tn(x_k, dul_k)
    full_down = tn(act_k, dy_k)
    mixture_part = jnp.zeros((width,), f32)
    query_part = jnp.zeros((cols,), f32)
    key_part = jnp.zeros((cols,), f32)
    x_own = tokens.astype(f32)
    own_scale = inverse_rms(x_own)
    dh_rows = []
    dqkv_rows = []
    d_hiddens = []
    input_grads = []
    for m in range(micro):
        db = db_list[m].astype(f32)
        mixture_part = mixture_part + jnp.sum(db * h_n[m], axis=0)
        w_g = db * gain_mixture
        d_hidden = cotangent[m].astype(f32) + h_scale[m] * (
            w_g - h_n[m] * jnp.mean(w_g * h_n[m], axis=-1, keepdims=True)
        )
        dh_m = jnp.concatenate(gather_shard(d_hidden.astype(bf16)), axis=0)
        if m == 0:
            out_part = jnp.stack(out_parts, axis=1)
            dh_m, full_gate, full_up, full_down, out_part = tie(dh_m, full_gate, full_up, full_down, out_part)
        dh_rows.append(dh_m)
        w_q, w_k, d_v, part_q, part_k, sums = attend_back(
            m, dh_m, w_o, linear, q_r, k_r, v_r, lse, q_inv, k_inv, gain_query, gain_key, cosine, sine, ids, order, heads
        )
        query_part = query_part + part_q[0]
        key_part = key_part + part_k[0]
        sums = lax.all_gather(sums, "shard", axis=0)
        d_qkv = project_back(m, w_q, w_k, d_v, linear, q_inv, k_inv, sums, order)
        if m + 1 < micro:
            db_list[m + 1], d_qkv, out_part = tie(db_list[m + 1], d_qkv, out_part)
            out_own = lax.psum_scatter(out_part, "expert", scatter_dimension=0, tiled=True)[0]
        dqkv_rows.append(d_qkv)
        d_hiddens.append(d_hidden)
    dh_all = jnp.concatenate(dh_rows, axis=0)
    grad_wo = jnp.stack(
        [tn(o_all, dh_all[:, i * cols : (i + 1) * cols]).astype(bf16).reshape(owners, rows, cols) for i in range(4)],
        axis=1,
    ).reshape(width, cols)

    blank = jnp.zeros((width,), f32)
    gains = jnp.stack(
        [
            blank,
            lax.dynamic_update_slice(blank, query_part, (s_index * cols,)),
            lax.dynamic_update_slice(blank, key_part, (s_index * cols,)),
            mixture_part,
        ],
        axis=1,
    )
    (aux_grad,) = tie(
        jnp.concatenate([gains, router_part.T, jnp.zeros((width, aux_cols - 4 - experts), f32)], axis=1).astype(bf16)
    )
    grad_payload = jnp.concatenate([tn(a_all, jnp.concatenate(dqkv_rows, axis=0)).astype(bf16), grad_wo, aux_grad], axis=1)
    grad_payload, out_own, *dqkv_rows = tie(grad_payload, out_own, *dqkv_rows)
    grad_own = lax.psum_scatter(grad_payload, "expert", scatter_dimension=0, tiled=True)
    output = (hidden + out_own.astype(f32)).astype(bf16)
    for m in range(micro):
        da_part = nt(dqkv_rows[m], w_qkv)
        da_part = da_part.reshape(4, tok, width)
        da = scatter_shard([da_part[j] for j in range(4)])
        da, full_gate, full_up, full_down = tie(da, full_gate, full_up, full_down)
        x_n = x_own[m] * own_scale[m]
        a_g = da * gain_attention
        grad = d_hiddens[m] + own_scale[m] * (a_g - x_n * jnp.mean(a_g * x_n, axis=-1, keepdims=True))
        input_grads.append(grad.astype(bf16))
    input_grad = jnp.stack(input_grads)
    sent_gate = send_side(full_gate, side)
    sent_up = send_side(full_up, side)
    sent_down = send_side(full_down, side)
    grad_gate = share_expert_grad(full_gate, sent_gate, core, side)
    grad_up = share_expert_grad(full_up, sent_up, core, side)
    grad_down = share_expert_grad(full_down, sent_down, core, side)
    grad_own = grad_own.reshape(4, rows, 4 * cols + aux_cols)
    grad_wo = grad_own[:, :, 3 * cols : 4 * cols].transpose(1, 0, 2).reshape(rows, width)
    grad_wo = lax.ppermute(grad_wo, BOTH, [(d, b) for b, d in moves]).astype(f32)
    grad_own = jnp.concatenate([grad_own[:, :, : 3 * cols], grad_own[:, :, 4 * cols :]], axis=2)
    grad_own = lax.all_to_all(grad_own, "shard", split_axis=0, concat_axis=0, tiled=True).astype(f32)
    grad_q, grad_k, grad_v = [
        grad_own[:, :, i * cols : (i + 1) * cols].transpose(1, 0, 2).reshape(rows, width)
        for i in range(3)
    ]
    aux_sum = jnp.sum(grad_own[:, :, 3 * cols :], axis=0)
    grad_gain = sum(
        jnp.sum(w.astype(f32) * g, axis=1) for w, g in ((w_query, grad_q), (w_key, grad_k), (w_value, grad_v))
    )
    grad_gain = grad_gain / attention_gain.astype(f32)
    return (
        output,
        input_grad,
        grad_q,
        grad_k,
        grad_v,
        grad_wo,
        aux_sum[:, 4 : 4 + experts],
        grad_gain,
        aux_sum[:, 1],
        aux_sum[:, 2],
        aux_sum[:, 3],
        grad_gate,
        grad_up,
        grad_down,
    )


def solution(mesh):
    tokens_spec = P(None, BOTH, None)
    rows_spec = P(BOTH, None)
    gain_spec = P(BOTH)
    expert_spec = P("expert", "shard", None)
    return jax.shard_map(
        local,
        mesh=mesh,
        in_specs=(tokens_spec, tokens_spec, P(None, "expert", None), tokens_spec)
        + (rows_spec,) * 5
        + (gain_spec,) * 4
        + (expert_spec,) * 3,
        out_specs=(tokens_spec, tokens_spec)
        + (rows_spec,) * 5
        + (gain_spec,) * 4
        + (expert_spec,) * 3,
        check_vma=False,
    )
```
